512 devices in a mesh: dp: 32 (over y, x_lo, core), mp: 16 (over z, x_hi).
Axes of the slice: x: 4 (x_hi: 2, x_lo: 2; x = x_hi * 2 + x_lo), y: 8, z: 8, core: 2. Of those that a mesh axis runs over, the one named last changes fastest.
Arguments:
- hidden: bfloat16 [4096, 2048], P('dp', 'mp'), may hold values from -6 to 6
- q_weight: bfloat16 [2048, 3072], P('dp', 'mp'), may hold values from -0.125 to 0.125
- dkv_weight: bfloat16 [2048, 576], P('mp', 'dp'), may hold values from -0.125 to 0.125
- latent_gain: float32 [512], replicated, may hold values from 0.1 to 1.9
- kvb_weight: bfloat16 [512, 16, 256], P('dp', 'mp'), may hold values from -0.25 to 0.25
- out_weight: bfloat16 [2048, 2048], P('mp', 'dp'), may hold values from -0.125 to 0.125
- cache: bfloat16 [8192, 64, 576], P(('dp', 'mp')), may hold values from -200 to 200
- cache_len: int32 [64], P('dp'), may hold values from 64 to 8128
- draft_count: int32 [64], P('dp'), may hold values from 32 to 64
- parents: int32 [64, 64], P('dp'), may hold values from 0 to 62, as said below
- accept_node: int32 [64], P('dp'), may hold values from 0 to 63, as said below
- page_table: int32 [64, 128], P('dp'), may hold values from 0 to 255, as said below
Outputs:
- attended: bfloat16 [4096, 2048], P(('dp', 'mp'))
- new_cache: bfloat16 [8192, 64, 576], P(('dp', 'mp'))
The draws below stay inside these ranges and needn't reach their ends.
Inputs may be any that keep to these rules, and one draw needn't show every extreme that they name: `page_table`: within each group of 2 consecutive requests the entries are a permutation of 0 to 255; entry v is slot v % 16 of the group's device v // 16 along mp. parents[q, 0] = 0 and parents[q, i] < i for i >= 1. `accept_node`: less than the request's draft_count.
All inputs are finite; a program needn't handle non-finite values.
Results may differ from the reference program's by a relative error of at most 0.03.
Values may be sent and summed in bfloat16 or wider, within the bound.
No kernel may reach another device: no remote copies, remote signals or barrier semaphores. Data moves between devices by JAX's collectives and lax.ppermute only.
A program may use at most 64 MiB of HBM per device.

```python
import jax
import jax.numpy as jnp
from jax import lax

D = 2048
H = 16
NOPE = 128
ROPE = 64
VDIM = 128
LAT = 512
DRAFT = 64
PAGE = 64
MAXLEN = 8192
REQ_DP = 2
REQS = 64
TOKENS = 4096
MAXPAGES = 128
PAGES = 8192


def draw_cache(key, part):
    base = jnp.clip(jax.random.normal(key, (PAGES, PAGE, LAT + ROPE), jnp.float32), -5.0, 5.0)
    return base.astype(jnp.bfloat16)


def draw_cache_len(key, part):
    lengths = jax.random.randint(key, (REQS,), PAGE, MAXLEN - DRAFT + 1, dtype=jnp.int32)
    return lengths.at[0].set(MAXLEN - DRAFT)


def shared_counts(key):
    counts = jax.random.randint(jax.random.fold_in(key, 11), (REQS,), DRAFT // 2, DRAFT + 1, dtype=jnp.int32)
    return counts.at[0].set(DRAFT)


def draw_draft_count(key, part):
    return shared_counts(key)


def draw_accept_node(key, part):
    counts = shared_counts(key)
    accepted = jax.random.randint(jax.random.fold_in(key, 12), (REQS,), 0, counts, dtype=jnp.int32)
    accepted = accepted.at[0].set(DRAFT - 1)
    return accepted.at[1].set(0)


def draw_parents(key, part):
    backward = jax.random.randint(key, (REQS, DRAFT), 0, 4, dtype=jnp.int32)
    backward = backward.at[0, DRAFT - 1].set(0)
    index = jnp.arange(DRAFT, dtype=jnp.int32)[None, :]
    return jnp.maximum(index - 1 - backward, 0).astype(jnp.int32)


def draw_page_table(key, part):
    groups = REQS // REQ_DP
    group_keys = jax.random.split(key, groups)
    shuffled = jax.vmap(lambda group_key: jax.random.permutation(group_key, REQ_DP * MAXPAGES))(group_keys)
    return shuffled.reshape(REQS, MAXPAGES).astype(jnp.int32)


def steps_of(key, shape, cuts, smallest, high):
    gain, own = 1.0, jax.random.fold_in(key, 6)
    for dim, blocks in cuts:
        steps = jnp.exp(jax.random.uniform(jax.random.fold_in(own, dim), (blocks,), jnp.float32, smallest / len(cuts), high / len(cuts)))
        gain = gain * jnp.repeat(steps, shape[dim] // blocks).reshape([-1 if axis == dim else 1 for axis in range(len(shape))])
    return gain


def gaussian(rng, extent, deviation, limit, cuts=(), held_as=jnp.bfloat16):
    values = deviation * jax.random.normal(rng, extent, jnp.float32)
    if cuts:
        values = values * steps_of(rng, extent, cuts, -0.22, 0.18)
    return jnp.clip(values, -limit, limit).astype(held_as)


def setup_inputs(seed: int = 0) -> dict:
    arg_keys = jax.random.split(jax.random.key(seed), 13)
    return {
        "hidden": gaussian(arg_keys[0], (TOKENS, D), 1.0, 6.0, ((0, 32), (1, 16))),
        "q_weight": gaussian(arg_keys[1], (D, H * (NOPE + ROPE)), D ** -0.5, 0.125, ((0, 32), (1, 16))),
        "dkv_weight": gaussian(arg_keys[2], (D, LAT + ROPE), D ** -0.5, 0.125, ((0, 16), (1, 32))),
        "latent_gain": jnp.clip(1.0 + 0.18 * jax.random.normal(arg_keys[3], (LAT,), jnp.float32), 0.1, 1.9),
        "kvb_weight": gaussian(arg_keys[4], (LAT, H, NOPE + VDIM), LAT ** -0.5, 0.25, ((0, 32), (1, 16))),
        "out_weight": gaussian(arg_keys[5], (H * VDIM, D), (H * VDIM) ** -0.5, 0.125, ((0, 16), (1, 32))),
        "cache": draw_cache(jax.random.fold_in(arg_keys[12], 71), 0),
        "cache_len": draw_cache_len(jax.random.fold_in(arg_keys[12], 71), 0),
        "draft_count": draw_draft_count(jax.random.fold_in(arg_keys[12], 71), 0),
        "parents": draw_parents(jax.random.fold_in(arg_keys[12], 71), 0),
        "accept_node": draw_accept_node(jax.random.fold_in(arg_keys[12], 71), 0),
        "page_table": draw_page_table(jax.random.fold_in(arg_keys[12], 71), 0),
    }


def tree_reach(parent_row):
    count = parent_row.shape[0]
    index = jnp.arange(count, dtype=jnp.int32)
    linked = jnp.logical_or(parent_row[:, None] == index[None, :], index[:, None] == index[None, :]).astype(jnp.float32)
    for _ in range(max(1, (count - 1).bit_length())):
        linked = jnp.minimum(jnp.dot(linked, linked, precision=lax.Precision.HIGHEST), 1.0)
    return linked

def angles(positions, width):
    half_dim = width // 2
    inverse = 10000.0 ** (-(jnp.arange(half_dim, dtype=jnp.float32) * 2.0) / width)
    phase = positions[..., None] * inverse
    return (jnp.cos(phase), jnp.sin(phase))

def rotary(values, cosine, sine):
    half_dim = values.shape[-1] // 2
    first = values[..., :half_dim]
    second = values[..., half_dim:]
    return jnp.concatenate([first * cosine - second * sine, second * cosine + first * sine], axis=-1)

def reference(hidden, q_weight, dkv_weight, latent_gain, kvb_weight, out_weight, cache, cache_len, draft_count, parents, accept_node, page_table):
    highest = lax.Precision.HIGHEST
    width = LAT + ROPE
    scale_val = (NOPE + ROPE) ** (-0.5)
    group_of = jnp.arange(REQS, dtype=jnp.int32) // REQ_DP
    global_pages = (page_table + (group_of * (REQ_DP * MAXPAGES))[:, None]).astype(jnp.int32)
    key_maps = kvb_weight[:, :, :NOPE].astype(jnp.float32)
    value_maps = kvb_weight[:, :, NOPE:].astype(jnp.float32)
    tokens_by_req = hidden.reshape(REQS, DRAFT, D)

    def one_request(packed):
        x_rows, length, count, parent_row, accepted, pages = packed
        linked = tree_reach(parent_row)
        depth = lax.optimization_barrier(jnp.sum(linked, axis=1)) - 1.0
        positions = length.astype(jnp.float32) + depth
        cosine, sine = angles(positions, ROPE)
        query = jnp.dot(x_rows, q_weight, preferred_element_type=jnp.float32).astype(jnp.bfloat16).reshape(DRAFT, H, NOPE + ROPE)
        q_rope = rotary(query[..., NOPE:].astype(jnp.float32), cosine[:, None, :], sine[:, None, :])
        q_latent = jnp.einsum('thn,lhn->thl', query[..., :NOPE].astype(jnp.float32), key_maps, precision=highest)
        absorbed = jnp.concatenate([q_latent, q_rope], axis=-1).astype(jnp.bfloat16).reshape(DRAFT * H, width)
        compressed = jnp.dot(x_rows, dkv_weight, preferred_element_type=jnp.float32)
        latent = compressed[:, :LAT]
        normed = latent * lax.rsqrt(lax.optimization_barrier(jnp.mean(latent * latent, axis=-1, keepdims=True)) + 1e-06) * latent_gain
        fresh = jnp.concatenate([normed, rotary(compressed[:, LAT:], cosine, sine)], axis=-1).astype(jnp.bfloat16)
        keys = cache[pages].reshape(MAXPAGES * PAGE, width)
        scores_c = jnp.dot(absorbed, keys.T, preferred_element_type=jnp.float32) * scale_val
        live_c = (jnp.arange(MAXPAGES * PAGE, dtype=jnp.int32) < length)[None, :]
        scores_t = jnp.dot(absorbed, fresh.T, preferred_element_type=jnp.float32).reshape(DRAFT, H, DRAFT) * scale_val
        live_t = (linked > 0.5)[:, None, :]
        top_c = lax.optimization_barrier(jnp.max(jnp.where(live_c, scores_c, -1e+30), axis=1)).reshape(DRAFT, H)
        top = jnp.maximum(top_c, lax.optimization_barrier(jnp.max(jnp.where(live_t, scores_t, -1e+30), axis=2)))
        prob_c = jnp.where(live_c, jnp.exp(scores_c - top.reshape(DRAFT * H)[:, None]), 0.0)
        prob_t = jnp.where(live_t, jnp.exp(scores_t - top[..., None]), 0.0)
        total = lax.optimization_barrier(jnp.sum(prob_c, axis=1)).reshape(DRAFT, H) + lax.optimization_barrier(jnp.sum(prob_t, axis=2))
        out_lat = jnp.dot(prob_c.astype(jnp.bfloat16), keys[:, :LAT], preferred_element_type=jnp.float32)
        out_lat = out_lat + jnp.dot(prob_t.reshape(DRAFT * H, DRAFT).astype(jnp.bfloat16), fresh[:, :LAT], preferred_element_type=jnp.float32)
        out_v = jnp.einsum('thl,lhv->thv', out_lat.reshape(DRAFT, H, LAT), value_maps, precision=highest) / total[..., None]
        head_out = out_v.astype(jnp.bfloat16).reshape(DRAFT, H * VDIM)
        result = jnp.dot(head_out, out_weight, preferred_element_type=jnp.float32)
        result = jnp.where((jnp.arange(DRAFT, dtype=jnp.int32) < count)[:, None], result, 0.0).astype(jnp.bfloat16)
        path = linked[accepted]
        picker = jnp.logical_and(path[None, :] > 0.5, depth[None, :] == jnp.arange(DRAFT, dtype=jnp.int32)[:, None].astype(jnp.float32))
        entries = jnp.dot(picker.astype(jnp.bfloat16), fresh, preferred_element_type=jnp.float32).astype(jnp.bfloat16)
        return (result, entries, jnp.sum(path) - 1.0)
    attended, entries, deepest = lax.map(one_request, (tokens_by_req, cache_len, draft_count, parents, accept_node, global_pages))
    positions = (cache_len[:, None] + jnp.arange(DRAFT, dtype=jnp.int32)[None, :]).astype(jnp.int32)
    written = jnp.arange(DRAFT, dtype=jnp.int32)[None, :].astype(jnp.float32) <= deepest[:, None]
    page_ids = jnp.take_along_axis(global_pages, positions // PAGE, axis=1)
    offsets = positions % PAGE
    current = cache[page_ids, offsets]
    new_cache = cache.at[page_ids, offsets].set(jnp.where(written[..., None], entries, current))
    return (attended.reshape(TOKENS, D), new_cache)
```

```python
import jax
import jax.numpy as jnp
from jax import lax
from jax.experimental import pallas as pl
from jax.experimental.pallas import tpu as pltpu
from jax.sharding import Mesh, PartitionSpec as P

NOPE = 128
ROPE = 64
LAT = 512
WIDTH = LAT + ROPE
AXES = ("y", "xl", "c", "zh", "zl", "xh")
DP = ("y", "xl", "c")
MP = ("zh", "zl", "xh")
Z = ("zh", "zl")
SCALE2 = (NOPE + ROPE) ** (-0.5) * 1.4426950408889634
NEG = -1e30
BF = jnp.bfloat16
F32 = jnp.float32


def tree_reach(parent_row):
    count = parent_row.shape[0]
    index = jnp.arange(count, dtype=jnp.int32)
    linked = jnp.logical_or(
        parent_row[:, None] == index[None, :], index[:, None] == index[None, :]
    ).astype(F32)
    for _ in range(max(1, (count - 1).bit_length())):
        linked = jnp.minimum(
            jnp.dot(linked.astype(BF), linked.astype(BF), preferred_element_type=F32), 1.0
        )
    return linked


def swap(x, axis):
    return lax.ppermute(x, axis, [(0, 1), (1, 0)])


def both(x, axis):
    other = swap(x, axis)
    first = lax.axis_index(axis) == 0
    return jnp.stack([jnp.where(first, x, other), jnp.where(first, other, x)])


def split3(v):
    hi = v.astype(BF)
    rest = v - hi.astype(F32)
    mid = rest.astype(BF)
    low = (rest - mid.astype(F32)).astype(BF)
    return [hi.astype(F32), mid.astype(F32), low.astype(F32)]


def attn_kernel(q_ref, k1_ref, k2_ref, bias_ref, o_ref, vt_ref):
    half = k1_ref.shape[0]

    @pl.when(pl.program_id(0) == 0)
    def _():
        vt_ref[:, :half] = k1_ref[:, :LAT].T
        vt_ref[:, half:] = k2_ref[:, :LAT].T

    q = jnp.concatenate([q_ref[0, :WIDTH, :], q_ref[1, :WIDTH, :]], axis=1)
    b1 = bias_ref[:half, :]
    b2 = bias_ref[half:, :]
    s1 = jnp.dot(k1_ref[...], q, preferred_element_type=F32) * SCALE2
    s2 = jnp.dot(k2_ref[...], q, preferred_element_type=F32) * SCALE2
    s1 = s1 + jnp.concatenate([b1, b1], axis=1)
    s2 = s2 + jnp.concatenate([b2, b2], axis=1)
    top = jnp.maximum(jnp.max(s1, axis=0, keepdims=True), jnp.max(s2, axis=0, keepdims=True))
    p1 = jnp.exp2(s1 - top)
    p2 = jnp.exp2(s2 - top)
    total = jnp.sum(p1, axis=0, keepdims=True) + jnp.sum(p2, axis=0, keepdims=True)
    out = jnp.dot(vt_ref[:, :half], p1.astype(BF), preferred_element_type=F32)
    out = out + jnp.dot(vt_ref[:, half:], p2.astype(BF), preferred_element_type=F32)
    stats = jnp.concatenate(
        split3(top) + split3(total) + [jnp.zeros((10, top.shape[1]), F32)], axis=0
    ).astype(BF)
    out = out.astype(BF)
    for h in range(2):
        o_ref[h, :LAT, :] = out[:, h * 128 : (h + 1) * 128]
        o_ref[h, LAT:, :] = stats[:, h * 128 : (h + 1) * 128]


def attend(queries, keys1, keys2, bias):
    heads, rows, lanes = queries.shape
    n1 = keys1.shape[0]
    return pl.pallas_call(
        attn_kernel,
        grid=(heads // 2,),
        in_specs=[
            pl.BlockSpec((2, rows, lanes), lambda i: (i, 0, 0)),
            pl.BlockSpec((n1, WIDTH), lambda i: (0, 0)),
            pl.BlockSpec((n1, WIDTH), lambda i: (0, 0)),
            pl.BlockSpec((2 * n1, lanes), lambda i: (0, 0)),
        ],
        out_specs=pl.BlockSpec((2, LAT + 16, lanes), lambda i: (i, 0, 0)),
        out_shape=jax.ShapeDtypeStruct((heads, LAT + 16, lanes), BF),
        scratch_shapes=[pltpu.VMEM((LAT, 2 * n1), BF)],
        compiler_params=pltpu.CompilerParams(vmem_limit_bytes=48 * 1024 * 1024),
        name="cache_attention",
    )(queries, keys1, keys2, bias)


def merge_kernel(part_ref, q_ref, comp_ref, gain_ref, cos_ref, sin_ref, tb_ref, vt_ref, ow_ref, o_ref, f_ref):
    lat = comp_ref[:LAT, :]
    mean = jnp.mean(lat * lat, axis=0, keepdims=True)
    normed = lat * lax.rsqrt(mean + 1e-06) * gain_ref[...]
    first = comp_ref[LAT : LAT + ROPE // 2, :]
    second = comp_ref[LAT + ROPE // 2 :, :]
    cosine = cos_ref[...]
    sine = sin_ref[...]
    fresh32 = jnp.concatenate(
        [normed, first * cosine - second * sine, second * cosine + first * sine], axis=0
    )
    fresh_t = fresh32.astype(BF)
    fresh = fresh32.T.astype(BF)
    f_ref[...] = fresh
    scores = jnp.dot(fresh, q_ref[...], preferred_element_type=F32) * SCALE2 + tb_ref[...]
    top = jnp.max(scores, axis=0, keepdims=True)
    parts = part_ref.shape[0]
    tops = []
    sums = []
    for i in range(parts):
        stats = part_ref[i, LAT:, :].astype(F32)
        tops.append(stats[0:1] + stats[1:2] + stats[2:3])
        sums.append(stats[3:4] + stats[4:5] + stats[5:6])
        top = jnp.maximum(top, tops[i])
    weights = jnp.exp2(scores - top)
    total = jnp.sum(weights, axis=0, keepdims=True)
    acc = jnp.dot(fresh_t[:LAT], weights.astype(BF), preferred_element_type=F32)
    for i in range(parts):
        factor = jnp.exp2(tops[i] - top)
        total = total + sums[i] * factor
        acc = acc + part_ref[i, :LAT, :].astype(F32) * factor
    acc = (acc / total).astype(BF)
    head = jnp.dot(vt_ref[...], acc, preferred_element_type=F32)
    head = head.T.astype(BF)
    o_ref[...] = lax.dot_general(
        head, ow_ref[...], (((1,), (1,)), ((), ())), preferred_element_type=F32
    ).astype(BF)


def merge(parts, q_own, comp, gain, cosine, sine, tree_bias, value_t, out_t):
    tokens = q_own.shape[1]
    return pl.pallas_call(
        merge_kernel,
        out_shape=(
            jax.ShapeDtypeStruct((tokens, out_t.shape[0]), BF),
            jax.ShapeDtypeStruct((tokens, WIDTH), BF),
        ),
        compiler_params=pltpu.CompilerParams(vmem_limit_bytes=48 * 1024 * 1024),
        name="merge_project",
    )(parts, q_own, comp, gain, cosine, sine, tree_bias, value_t, out_t)


def per_device(
    hidden,
    q_weight,
    dkv_weight,
    latent_gain,
    kvb_weight,
    out_weight,
    cache,
    cache_len,
    draft_count,
    parents,
    accept_node,
    page_table,
):
    reqs, draft = parents.shape
    tokens = reqs * draft
    slots, page_len, width = cache.shape
    z_rank = lax.axis_index(Z)
    mp_rank = lax.axis_index(MP)
    keys = cache.reshape(slots * page_len, width)
    rows = jnp.concatenate([hidden, dkv_weight.T], axis=0)
    pair = both(rows, "xh")
    keys_other = swap(keys, "xh")
    hid = jnp.concatenate([pair[0, :tokens], pair[1, :tokens]], axis=1)
    cols = dkv_weight.shape[1]
    pack = jnp.concatenate(
        [
            q_weight[:, :NOPE],
            jnp.concatenate([q_weight[:32, NOPE:], q_weight[32:, NOPE:]], axis=1),
            kvb_weight[:, 0, :NOPE],
            kvb_weight[:, 0, NOPE:],
            out_weight.T,
            pair[0, tokens:],
            pair[1, tokens:],
            jnp.zeros((12, 128), BF),
        ],
        axis=0,
    )
    wide = lax.all_to_all(jnp.broadcast_to(pack[None], (8,) + pack.shape), "y", 0, 0, tiled=True)
    wide = both(both(wide, "xl"), "c")
    wide = wide.transpose(2, 1, 0, 3, 4)
    w_plain = wide[..., :64, :].reshape(2048, 128)
    w_rot = wide[..., 64:96, :]
    w_rot = jnp.concatenate([w_rot, w_rot], axis=3).reshape(2048, 128)
    key_map = wide[..., 96:112, :].reshape(LAT, NOPE)
    value_t = wide[..., 112:128, :].reshape(LAT, 128).T
    out_t = wide[..., 128:192, :].reshape(2048, 128)
    down = jnp.concatenate(
        [wide[..., 192 : 192 + cols, :], wide[..., 192 + cols : 192 + 2 * cols, :]], axis=4
    ).reshape(8, 4 * cols, 256)
    sent = jnp.concatenate([jnp.broadcast_to(hid[None], (8,) + hid.shape), down], axis=1)
    got = lax.all_to_all(sent, Z, 0, 0, tiled=True)
    full_x = got[:, :tokens].transpose(1, 0, 2).reshape(tokens, 2048)
    down_t = got[:, tokens:].transpose(1, 0, 2).reshape(4 * cols, 2048)
    linked = jax.vmap(tree_reach)(parents)
    depth = jnp.sum(linked, axis=2) - 1.0
    positions = (cache_len.astype(F32)[:, None] + depth).reshape(1, tokens)
    inverse = 10000.0 ** (-(jnp.arange(ROPE // 2, dtype=F32) * 2.0) / ROPE)
    phase = positions * inverse[:, None]
    cosine = jnp.cos(phase)
    sine = jnp.sin(phase)
    q_plain = jnp.dot(full_x, w_plain, preferred_element_type=F32).astype(BF)
    early = (jnp.arange(2048) % 64 < 32)[None, :]
    zero = jnp.zeros((), BF)
    rot_a = jnp.dot(jnp.where(early, full_x, zero), w_rot, preferred_element_type=F32)
    rot_b = jnp.dot(jnp.where(early, zero, full_x), w_rot, preferred_element_type=F32)
    q_rot = (rot_a[:, :ROPE] + rot_b[:, ROPE:]).T.astype(BF).astype(F32)
    q_lat = lax.dot_general(
        key_map, q_plain, (((1,), (1,)), ((), ())), preferred_element_type=F32
    )
    r1 = q_rot[: ROPE // 2]
    r2 = q_rot[ROPE // 2 :]
    q_own = jnp.concatenate(
        [q_lat, r1 * cosine - r2 * sine, r2 * cosine + r1 * sine], axis=0
    ).astype(BF)
    comp = lax.dot_general(
        down_t, full_x, (((1,), (1,)), ((), ())), preferred_element_type=F32
    ).astype(BF)
    packed = jnp.concatenate([q_own, comp, jnp.zeros((8, tokens), BF)], axis=0)
    queries = lax.all_to_all(
        jnp.broadcast_to(packed[None], (8,) + packed.shape), Z, 0, 0, tiled=True
    )
    slot_base = jnp.stack([mp_rank, mp_rank ^ 1]) * slots
    slot_ids = (slot_base[:, None] + jnp.arange(slots, dtype=jnp.int32)[None, :]).reshape(-1)
    page_ids = jnp.arange(reqs * page_table.shape[1], dtype=jnp.int32)
    place = jnp.sum(
        jnp.where(page_table.reshape(-1)[:, None] == slot_ids[None, :], page_ids[:, None], 0), axis=0
    )
    slot_req = place // page_table.shape[1]
    slot_page = place % page_table.shape[1]
    token_req = jnp.arange(tokens, dtype=jnp.int32) // draft
    token_len = jnp.repeat(cache_len, draft)
    key_pos = slot_page[:, None] * page_len + jnp.arange(page_len, dtype=jnp.int32)[None, :]
    same = slot_req[:, None, None] == token_req[None, None, :]
    offset = key_pos[:, :, None] - token_len[None, None, :]
    bias = jnp.where(jnp.logical_and(same, offset < 0), 0.0, NEG).astype(F32)
    bias = bias.reshape(2 * slots * page_len, tokens)
    accept_hot = (accept_node[:, None] == jnp.arange(draft, dtype=jnp.int32)[None, :]).astype(F32)
    path = jnp.sum(accept_hot[:, :, None] * linked, axis=1).reshape(tokens)
    write_at = jnp.where(path > 0.5, depth.reshape(tokens).astype(jnp.int32), -1)
    chosen = jnp.logical_and(
        same[:slots],
        jnp.logical_and(write_at[None, None, :] >= 0, offset[:slots] == write_at[None, None, :]),
    )
    chosen = chosen.reshape(slots * page_len, tokens).astype(BF)
    partial = attend(queries, keys, keys_other, bias)
    partial = lax.all_to_all(partial, Z, 0, 0, tiled=True)
    comp_all = queries[:, WIDTH : WIDTH + 4 * cols].reshape(WIDTH, tokens).astype(F32)
    linked_t = linked.transpose(0, 2, 1)
    blank = jnp.zeros((draft, draft), F32)
    tree_live = jnp.concatenate(
        [
            jnp.concatenate([linked_t[0], blank], axis=1),
            jnp.concatenate([blank, linked_t[1]], axis=1),
        ],
        axis=0,
    )
    tree_bias = jnp.where(tree_live > 0.5, 0.0, NEG).astype(F32)
    gain = jnp.broadcast_to(latent_gain[:, None], (LAT, tokens))
    projected, fresh = merge(
        partial, q_own, comp_all, gain, cosine, sine, tree_bias, value_t, out_t
    )
    shares = lax.all_to_all(projected.reshape(16, tokens // 16, 2048), MP, 0, 0, tiled=True)
    mine_rows = jnp.sum(shares.astype(F32), axis=0)
    row_index = mp_rank * (tokens // 16) + jnp.arange(tokens // 16, dtype=jnp.int32)
    row_count = jnp.sum(
        jnp.where(
            (row_index // draft)[:, None] == jnp.arange(reqs, dtype=jnp.int32)[None, :],
            draft_count[None, :],
            0,
        ),
        axis=1,
    )
    attended = jnp.where((row_index % draft < row_count)[:, None], mine_rows, 0.0).astype(BF)
    placed = jnp.dot(chosen, fresh, preferred_element_type=F32).astype(BF)
    written = jnp.sum(chosen.astype(F32), axis=1, keepdims=True) > 0.5
    new_cache = jnp.where(written, placed, keys).reshape(cache.shape)
    return (attended, new_cache)


def solution(mesh):
    grid = Mesh(mesh.devices.reshape(8, 2, 2, 2, 4, 2), AXES)
    return jax.shard_map(
        per_device,
        mesh=grid,
        in_specs=(
            P(DP, MP),
            P(DP, MP),
            P(MP, DP),
            P(),
            P(DP, MP, None),
            P(MP, DP),
            P(DP + MP, None, None),
            P(DP),
            P(DP),
            P(DP, None),
            P(DP),
            P(DP, None),
        ),
        out_specs=(P(DP + MP, None), P(DP + MP, None, None)),
        check_vma=False,
    )
```

```python
import jax
import jax.numpy as jnp
from jax import lax
from jax.experimental import pallas as pl
from jax.experimental.pallas import tpu as pltpu
from jax.sharding import Mesh, PartitionSpec as P

NOPE = 128
ROPE = 64
LAT = 512
WIDTH = LAT + ROPE
AXES = ("y", "xl", "c", "zh", "zl", "xh")
DP = ("y", "xl", "c")
MP = ("zh", "zl", "xh")
Z = ("zh", "zl")
SIDE = 80
SCALE2 = (NOPE + ROPE) ** (-0.5) * 1.4426950408889634
NEG = -1e30
BF = jnp.bfloat16
F32 = jnp.float32


def tree_reach(parent_row):
    count = parent_row.shape[0]
    index = jnp.arange(count, dtype=jnp.int32)
    linked = jnp.logical_or(
        parent_row[:, None] == index[None, :], index[:, None] == index[None, :]
    ).astype(F32)
    for _ in range(max(1, (count - 1).bit_length())):
        linked = jnp.minimum(
            jnp.dot(linked.astype(BF), linked.astype(BF), preferred_element_type=F32), 1.0
        )
    return linked


def swap(x, axis):
    return lax.ppermute(x, axis, [(0, 1), (1, 0)])


def both(x, axis):
    other = swap(x, axis)
    first = lax.axis_index(axis) == 0
    return jnp.stack([jnp.where(first, x, other), jnp.where(first, other, x)])


def split3(v):
    hi = v.astype(BF)
    rest = v - hi.astype(F32)
    mid = rest.astype(BF)
    low = (rest - mid.astype(F32)).astype(BF)
    return [hi.astype(F32), mid.astype(F32), low.astype(F32)]


def prep_kernel(k1_ref, k2t_ref, mask_ref, k_ref, v_ref):
    half = k1_ref.shape[0]
    k_ref[:half, :WIDTH] = k1_ref[...]
    k_ref[half:, :WIDTH] = k2t_ref[...].T
    k_ref[:, WIDTH:] = mask_ref[...]
    v_ref[:, :half] = k1_ref[:, :LAT].T
    v_ref[:, half:] = k2t_ref[:LAT, :]


def prepare(keys, other_t, mask):
    n1 = keys.shape[0]
    return pl.pallas_call(
        prep_kernel,
        out_shape=(
            jax.ShapeDtypeStruct((2 * n1, WIDTH + 16), BF),
            jax.ShapeDtypeStruct((LAT, 2 * n1), BF),
        ),
        compiler_params=pltpu.CompilerParams(vmem_limit_bytes=48 * 1024 * 1024),
        name="prepare_keys",
    )(keys, other_t, mask)


def maps_kernel(w_ref, km_ref, vm_ref):
    order = [(y, xl, c) for y in range(8) for xl in range(2) for c in range(2)]
    for h in range(8):
        for n, (y, xl, c) in enumerate(order):
            km_ref[h, 16 * n : 16 * n + 16, :] = w_ref[c, xl, y, 16 * h : 16 * h + 16, :]
        value = [w_ref[c, xl, y, 128 + 16 * h : 144 + 16 * h, :] for y, xl, c in order]
        vm_ref[h] = jnp.concatenate(value, axis=0).T


def arrange(wide):
    return pl.pallas_call(
        maps_kernel,
        out_shape=(
            jax.ShapeDtypeStruct((8, LAT, 128), BF),
            jax.ShapeDtypeStruct((8, 128, LAT), BF),
        ),
        compiler_params=pltpu.CompilerParams(vmem_limit_bytes=48 * 1024 * 1024),
        name="arrange_maps",
    )(wide)


def project_kernel(x_ref, w_ref, h_ref, d_ref, cos_ref, sin_ref, o_ref):
    tokens = h_ref.shape[0]
    nt = (((1,), (1,)), ((), ()))
    part = lax.dot_general(h_ref[...], d_ref[...], nt, preferred_element_type=F32)
    part = jnp.concatenate([part, jnp.zeros((tokens, ROPE), F32)], axis=1).astype(BF)
    order = [(0, 0), (1, 0), (0, 1), (1, 1)]
    zero = jnp.zeros((32, 128), BF)
    acc = jnp.zeros((tokens, 3 * 128), F32)
    for y in range(8):
        plain = []
        rot_a = []
        rot_b = []
        for c, xl in order:
            plain.append(w_ref[c, xl, y, 0:64, :])
            rot = w_ref[c, xl, y, 64:96, :]
            rot_a += [rot, zero]
            rot_b += [zero, rot]
        weights = jnp.concatenate(
            [
                jnp.concatenate(plain, axis=0),
                jnp.concatenate(rot_a, axis=0),
                jnp.concatenate(rot_b, axis=0),
            ],
            axis=1,
        )
        acc = acc + jnp.dot(x_ref[y, :tokens], weights, preferred_element_type=F32)
    q_plain = acc[:, :128].T
    rot = acc[:, 128:256].T[:ROPE] + acc[:, 256:384].T[ROPE:]
    rot = rot.astype(BF).astype(F32)
    r1 = rot[: ROPE // 2]
    r2 = rot[ROPE // 2 :]
    cosine = cos_ref[...]
    sine = sin_ref[...]
    q_rot = jnp.concatenate([r1 * cosine - r2 * sine, r2 * cosine + r1 * sine], axis=0)
    lane = lax.broadcasted_iota(jnp.int32, (16, tokens), 1) // (tokens // 2)
    row = lax.broadcasted_iota(jnp.int32, (16, tokens), 0)
    which = jnp.where(lane == row, 1.0, 0.0)
    tail = jnp.concatenate([q_plain, q_rot, which], axis=0).astype(BF)
    for i in range(o_ref.shape[0]):
        for k in range(5):
            o_ref[i, 16 * k : 16 * k + 16, :] = part[16 * i : 16 * i + 16, 128 * k : 128 * k + 128]
        o_ref[i, SIDE:, :] = tail


def project(x, wide, own, down, cosine, sine):
    tokens = own.shape[0]
    return pl.pallas_call(
        project_kernel,
        out_shape=jax.ShapeDtypeStruct((8, SIDE + NOPE + ROPE + 16, tokens), BF),
        compiler_params=pltpu.CompilerParams(vmem_limit_bytes=48 * 1024 * 1024),
        name="project_queries",
    )(x, wide, own, down, cosine, sine)


def attn_kernel(q_ref, k_ref, v_ref, km_ref, vm_ref, part_ref, gain_ref, cos_ref, sin_ref, o_ref):
    comp = jnp.zeros((SIDE, 128), F32)
    for i in range(part_ref.shape[0]):
        for j in range(part_ref.shape[1]):
            comp = comp + part_ref[i, j].astype(F32)
    squares = jnp.zeros((16, 128), F32)
    for k in range(4):
        lat = comp[16 * k : 16 * k + 16]
        squares = squares + lat * lat
    scale = lax.rsqrt(jnp.sum(squares, axis=1, keepdims=True) * (1.0 / LAT) + 1e-06)
    fresh = [
        comp[16 * k : 16 * k + 16] * scale * gain_ref[:, 128 * k : 128 * k + 128] for k in range(4)
    ]
    rot = comp[64:80]
    lane = lax.broadcasted_iota(jnp.int32, rot.shape, 1)
    across = jnp.where(lane < 32, pltpu.roll(rot, 96, 1), pltpu.roll(rot, 32, 1))
    fresh.append(rot * cos_ref[...] + across * sin_ref[...])
    fresh = jnp.concatenate(fresh, axis=0).astype(BF)
    q = []
    for h in range(2):
        lat = jnp.dot(
            km_ref[h, 0], q_ref[h, 0, SIDE : SIDE + NOPE, :], preferred_element_type=F32
        ).astype(BF)
        q.append(jnp.concatenate([lat, q_ref[h, 0, SIDE + NOPE :, :]], axis=0))
    q = jnp.concatenate(q, axis=1)
    scores = jnp.dot(k_ref[...], q, preferred_element_type=F32)
    top = jnp.max(scores, axis=0, keepdims=True) * SCALE2
    weights = jnp.exp2(scores * SCALE2 - top)
    total = jnp.sum(weights, axis=0, keepdims=True)
    out = jnp.dot(v_ref[...], weights.astype(BF), preferred_element_type=F32).astype(BF)
    a = jnp.dot(vm_ref[0, 0], out[:, :128], preferred_element_type=F32)
    b = jnp.dot(vm_ref[1, 0], out[:, 128:], preferred_element_type=F32)
    stats = jnp.concatenate(
        split3(top) + split3(total) + [jnp.zeros((10, top.shape[1]), F32)], axis=0
    )
    a = jnp.concatenate([a, stats[:, :128]], axis=0)
    b = jnp.concatenate([b, stats[:, 128:]], axis=0)
    low = lax.broadcasted_iota(jnp.int32, a.shape, 1) < 64
    rows = a.shape[0]
    o_ref[0, 0, :rows, :] = jnp.where(low, a, pltpu.roll(b, 64, 1)).astype(BF)
    o_ref[1, 0, :rows, :] = jnp.where(low, pltpu.roll(a, 64, 1), b).astype(BF)
    o_ref[0, 0, rows:, :] = fresh
    o_ref[1, 0, rows:, :] = fresh


def attend(queries, keys, values_t, key_maps, value_maps, gain, cosine, sine):
    groups, pairs, rows, lanes = queries.shape
    n = keys.shape[0]
    out_rows = 128 + 16 + SIDE
    return pl.pallas_call(
        attn_kernel,
        grid=(pairs,),
        in_specs=[
            pl.BlockSpec((2, 1, rows, lanes), lambda i: (0, i, 0, 0)),
            pl.BlockSpec((n, WIDTH + 16), lambda i: (0, 0)),
            pl.BlockSpec((LAT, n), lambda i: (0, 0)),
            pl.BlockSpec((2, 1, LAT, 128), lambda i: (0, i, 0, 0)),
            pl.BlockSpec((2, 1, 128, LAT), lambda i: (0, i, 0, 0)),
            pl.BlockSpec((groups, pairs, SIDE, lanes), lambda i: (0, 0, 0, 0)),
            pl.BlockSpec((1, LAT), lambda i: (0, 0)),
            pl.BlockSpec((16, 128), lambda i: (0, 0)),
            pl.BlockSpec((16, 128), lambda i: (0, 0)),
        ],
        out_specs=pl.BlockSpec((2, 1, out_rows, lanes), lambda i: (0, i, 0, 0)),
        out_shape=jax.ShapeDtypeStruct((2, pairs, out_rows, lanes), BF),
        compiler_params=pltpu.CompilerParams(vmem_limit_bytes=48 * 1024 * 1024),
        name="cache_attention",
    )(queries, keys, values_t, key_maps, value_maps, queries, gain, cosine, sine)


def merge_kernel(part_ref, q_ref, km_ref, vm_ref, tb_ref, w_ref, o_ref, f_ref):
    parts = part_ref.shape[0]
    base = 128 + 16
    fresh = jnp.concatenate(
        [
            jnp.concatenate(
                [part_ref[i, base + 16 * k : base + 16 * k + 16, :] for k in range(5)], axis=1
            )
            for i in range(parts)
        ],
        axis=0,
    )
    fresh_t = fresh[:, :LAT].astype(F32).T.astype(BF)
    fresh = fresh[:, :WIDTH]
    f_ref[...] = fresh
    low = lax.broadcasted_iota(jnp.int32, (1, q_ref.shape[1]), 1) < 64
    plain = q_ref[:NOPE]
    lat = [jnp.dot(km_ref[h], plain, preferred_element_type=F32) for h in range(2)]
    lat = jnp.where(low, lat[0], lat[1]).astype(BF)
    q = jnp.concatenate([lat, q_ref[NOPE:]], axis=0)
    scores = jnp.dot(fresh, q, preferred_element_type=F32) * SCALE2 + tb_ref[...]
    top = jnp.max(scores, axis=0, keepdims=True)
    tops = []
    sums = []
    for i in range(parts):
        stats = part_ref[i, 128 : 128 + 16, :].astype(F32)
        tops.append(stats[0:1] + stats[1:2] + stats[2:3])
        sums.append(stats[3:4] + stats[4:5] + stats[5:6])
        top = jnp.maximum(top, tops[i])
    weights = jnp.exp2(scores - top)
    total = jnp.sum(weights, axis=0, keepdims=True)
    tree = jnp.dot(fresh_t, weights.astype(BF), preferred_element_type=F32).astype(BF)
    tree = [jnp.dot(vm_ref[h], tree, preferred_element_type=F32) for h in range(2)]
    acc = jnp.where(low, tree[0], tree[1])
    for i in range(parts):
        factor = jnp.exp2(tops[i] - top)
        total = total + sums[i] * factor
        acc = acc + part_ref[i, :128, :].astype(F32) * factor
    head = (acc / total).T.astype(BF)
    n = head.shape[0] // 2
    blocks = w_ref.shape[0]
    result = jnp.zeros((n, blocks * 64), F32)
    for h in range(2):
        project = w_ref[:, 64 * h : 64 * (h + 1), :].reshape(blocks * 64, 128)
        result = result + lax.dot_general(
            head[h * n : (h + 1) * n],
            project,
            (((1,), (1,)), ((), ())),
            preferred_element_type=F32,
        )
    o_ref[...] = result.astype(BF)


def merge(parts, q_pair, key_maps, value_maps, tree_bias, late):
    lanes = q_pair.shape[1]
    return pl.pallas_call(
        merge_kernel,
        out_shape=(
            jax.ShapeDtypeStruct((lanes // 2, late.shape[0] * 64), BF),
            jax.ShapeDtypeStruct((tree_bias.shape[0], WIDTH), BF),
        ),
        compiler_params=pltpu.CompilerParams(vmem_limit_bytes=48 * 1024 * 1024),
        name="merge_project",
    )(parts, q_pair, key_maps, value_maps, tree_bias, late)


def per_device(
    hidden,
    q_weight,
    dkv_weight,
    latent_gain,
    kvb_weight,
    out_weight,
    cache,
    cache_len,
    draft_count,
    parents,
    accept_node,
    page_table,
):
    reqs, draft = parents.shape
    tokens = reqs * draft
    slots, page_len, width = cache.shape
    mp_rank = lax.axis_index(MP)
    zh = lax.axis_index("zh")
    zl = lax.axis_index("zl")
    cols = dkv_weight.shape[1]
    keys = cache.reshape(slots * page_len, width)
    pair = both(jnp.concatenate([hidden, dkv_weight.T], axis=0), "xh")
    hid = jnp.concatenate([pair[0, :tokens], pair[1, :tokens]], axis=1)
    pack = jnp.concatenate(
        [
            q_weight[:, :NOPE],
            jnp.concatenate([q_weight[:32, NOPE:], q_weight[32:, NOPE:]], axis=1),
            pair[0, tokens:],
            pair[1, tokens:],
            jnp.zeros((12, 128), BF),
        ],
        axis=0,
    )
    wide = lax.all_to_all(jnp.broadcast_to(pack[None], (8,) + pack.shape), "y", 0, 0, tiled=True)
    keys_t, late, hid = lax.optimization_barrier((keys.T, out_weight.T, hid))
    other_t = swap(keys_t, "xh")
    late = both(late, "zh").reshape(128, 128)
    sent = jnp.concatenate([hid, kvb_weight[:, 0, :]], axis=0)
    sent = jnp.broadcast_to(sent[None], (8,) + sent.shape)
    wide, sent, late = lax.optimization_barrier((wide, sent, late))
    full_x = lax.all_to_all(sent, Z, 0, 0, tiled=True)
    late = lax.all_gather(late, DP)
    wide = both(both(wide, "xl"), "c")
    wide, other_t = lax.optimization_barrier((wide, other_t))
    down = wide[..., 96 : 96 + 2 * cols, :].transpose(2, 1, 0, 3, 4).reshape(32, 2, cols, 128)
    down = jnp.concatenate([down[:, 0], down[:, 1]], axis=2).reshape(WIDTH, 256)
    maps = full_x[:, tokens:]
    maps = jnp.concatenate(
        [maps[..., :NOPE].reshape(128, 128), maps[..., NOPE:].reshape(128, 128)], axis=0
    )
    maps = lax.all_to_all(jnp.broadcast_to(maps[None], (8,) + maps.shape), "y", 0, 0, tiled=True)
    linked = jax.vmap(tree_reach)(parents)
    depth = jnp.sum(linked, axis=2) - 1.0
    positions = (cache_len.astype(F32)[:, None] + depth).reshape(1, tokens)
    inverse = 10000.0 ** (-(jnp.arange(ROPE // 2, dtype=F32) * 2.0) / ROPE)
    phase = positions * inverse[:, None]
    cosine = jnp.cos(phase)
    sine = jnp.sin(phase)
    mine = lax.dynamic_slice_in_dim(positions.reshape(tokens), 16 * (zh * 4 + zl), 16)
    mine = mine[:, None] * jnp.concatenate([inverse, inverse])[None, :]
    sign = jnp.where(jnp.arange(ROPE) < ROPE // 2, -1.0, 1.0)[None, :]
    mine_cos = jnp.pad(jnp.cos(mine), ((0, 0), (0, 128 - ROPE)))
    mine_sin = jnp.pad(jnp.sin(mine) * sign, ((0, 0), (0, 128 - ROPE)))
    queries = project(full_x, wide, hid, down, cosine, sine)
    queries, maps, other_t = lax.optimization_barrier((queries, maps, other_t))
    queries = lax.all_to_all(queries, Z, 0, 0, tiled=True)
    queries, late = lax.optimization_barrier((queries, late))
    maps = both(both(maps, "xl"), "c")
    slot_base = jnp.stack([mp_rank, mp_rank ^ 1]) * slots
    slot_ids = (slot_base[:, None] + jnp.arange(slots, dtype=jnp.int32)[None, :]).reshape(-1)
    page_ids = jnp.arange(reqs * page_table.shape[1], dtype=jnp.int32)
    place = jnp.sum(
        jnp.where(page_table.reshape(-1)[:, None] == slot_ids[None, :], page_ids[:, None], 0), axis=0
    )
    slot_req = place // page_table.shape[1]
    slot_page = place % page_table.shape[1]
    key_pos = slot_page[:, None] * page_len + jnp.arange(page_len, dtype=jnp.int32)[None, :]
    column = jnp.arange(16, dtype=jnp.int32)
    column_len = jnp.pad(cache_len, (0, 16 - reqs))
    hidden_key = jnp.logical_or(
        slot_req[:, None, None] != column, key_pos[:, :, None] >= column_len
    )
    mask = jnp.where(jnp.logical_and(hidden_key, column < reqs), NEG, 0.0).astype(BF)
    mask = mask.reshape(2 * slots * page_len, 16)
    token_req = jnp.arange(tokens, dtype=jnp.int32) // draft
    accept_hot = (accept_node[:, None] == jnp.arange(draft, dtype=jnp.int32)[None, :]).astype(F32)
    path = jnp.sum(accept_hot[:, :, None] * linked, axis=1)
    write_at = jnp.where(
        path > 0.5, cache_len[:, None] + depth.astype(jnp.int32), -1
    ).reshape(tokens)
    chosen = jnp.logical_and(
        slot_req[:slots, None, None] == token_req, key_pos[:slots, :, None] == write_at
    )
    chosen = chosen.reshape(slots * page_len, tokens).astype(BF)
    all_keys, values_t = prepare(keys, other_t, mask)
    key_maps, value_maps = arrange(maps)
    queries = queries.reshape((2, 4) + queries.shape[1:])
    key_maps = key_maps.reshape((2, 4) + key_maps.shape[1:])
    value_maps = value_maps.reshape((2, 4) + value_maps.shape[1:])
    partial = attend(
        queries, all_keys, values_t, key_maps, value_maps, latent_gain[None, :], mine_cos, mine_sin
    )
    partial = lax.all_to_all(
        partial.reshape((8,) + partial.shape[2:]), Z, 0, 0, tiled=True
    )
    q_pair = lax.dynamic_index_in_dim(queries, zl, 1, keepdims=False)
    q_pair = q_pair[:, SIDE : SIDE + NOPE + ROPE]
    q_pair = jnp.where(zh == 0, q_pair[..., :draft], q_pair[..., draft:])
    q_pair = jnp.concatenate([q_pair[0], q_pair[1]], axis=1)
    linked_t = jnp.where(zh == 0, linked[0], linked[1]).T
    blank = jnp.zeros((draft, draft), F32)
    live = jnp.concatenate(
        [jnp.where(zh == 0, linked_t, blank), jnp.where(zh == 0, blank, linked_t)], axis=0
    )
    tree_bias = jnp.where(jnp.concatenate([live, live], axis=1) > 0.5, 0.0, NEG).astype(F32)
    key_pair = lax.dynamic_index_in_dim(key_maps, zl, 1, keepdims=False)
    value_pair = lax.dynamic_index_in_dim(value_maps, zl, 1, keepdims=False)
    projected, fresh = merge(partial, q_pair, key_pair, value_pair, tree_bias, late)
    rows = tokens // 16
    shares = lax.all_to_all(projected.reshape(8, rows, 2048), ("zl", "xh"), 0, 0, tiled=True)
    mine_rows = jnp.sum(shares.astype(F32), axis=0)
    row_index = (mp_rank * rows) % draft + jnp.arange(rows, dtype=jnp.int32)
    row_count = jnp.where(zh == 0, draft_count[0], draft_count[1])
    attended = jnp.where((row_index < row_count)[:, None], mine_rows, 0.0).astype(BF)
    placed = jnp.dot(chosen, fresh, preferred_element_type=F32).astype(BF)
    written = jnp.sum(chosen.astype(F32), axis=1, keepdims=True) > 0.5
    new_cache = jnp.where(written, placed, keys).reshape(cache.shape)
    return (attended, new_cache)


def solution(mesh):
    grid = Mesh(mesh.devices.reshape(8, 2, 2, 2, 4, 2), AXES)
    return jax.shard_map(
        per_device,
        mesh=grid,
        in_specs=(
            P(DP, MP),
            P(DP, MP),
            P(MP, DP),
            P(),
            P(DP, MP, None),
            P(MP, DP),
            P(DP + MP, None, None),
            P(DP),
            P(DP),
            P(DP, None),
            P(DP),
            P(DP, None),
        ),
        out_specs=(P(DP + MP, None), P(DP + MP, None, None)),
        check_vma=False,
    )
```

```python
import jax
import jax.numpy as jnp
from jax import lax
from jax.experimental import pallas as pl
from jax.experimental.pallas import tpu as pltpu
from jax.sharding import Mesh, PartitionSpec as P

NOPE = 128
ROPE = 64
LAT = 512
WIDTH = LAT + ROPE
AXES = ("y", "xl", "c", "zh", "zl", "xh")
DP = ("y", "xl", "c")
MP = ("zh", "zl", "xh")
Z = ("zh", "zl")
SIDE = 80
SCALE2 = (NOPE + ROPE) ** (-0.5) * 1.4426950408889634
NEG = -1e30
BF = jnp.bfloat16
F32 = jnp.float32


def tree_reach(parent_row):
    count = parent_row.shape[0]
    index = jnp.arange(count, dtype=jnp.int32)
    linked = jnp.logical_or(
        parent_row[:, None] == index[None, :], index[:, None] == index[None, :]
    ).astype(F32)
    for _ in range(max(1, (count - 1).bit_length())):
        linked = jnp.minimum(
            jnp.dot(linked.astype(BF), linked.astype(BF), preferred_element_type=F32), 1.0
        )
    return linked


def swap(x, axis):
    return lax.ppermute(x, axis, [(0, 1), (1, 0)])


def both(x, axis):
    other = swap(x, axis)
    first = lax.axis_index(axis) == 0
    return jnp.stack([jnp.where(first, x, other), jnp.where(first, other, x)])


def split3(v):
    hi = v.astype(BF)
    rest = v - hi.astype(F32)
    mid = rest.astype(BF)
    low = (rest - mid.astype(F32)).astype(BF)
    return [hi.astype(F32), mid.astype(F32), low.astype(F32)]


def prep_kernel(k1_ref, k2t_ref, mask_ref, k_ref, v_ref):
    half = k1_ref.shape[0]
    k_ref[:half, :WIDTH] = k1_ref[...]
    k_ref[half:, :WIDTH] = k2t_ref[...].T
    k_ref[:, WIDTH:] = mask_ref[...]
    v_ref[:, :half] = k1_ref[:, :LAT].T
    v_ref[:, half:] = k2t_ref[:LAT, :]


def prepare(keys, other_t, mask):
    n1 = keys.shape[0]
    return pl.pallas_call(
        prep_kernel,
        out_shape=(
            jax.ShapeDtypeStruct((2 * n1, WIDTH + 16), BF),
            jax.ShapeDtypeStruct((LAT, 2 * n1), BF),
        ),
        compiler_params=pltpu.CompilerParams(vmem_limit_bytes=48 * 1024 * 1024),
        name="prepare_keys",
    )(keys, other_t, mask)


def maps_kernel(w_ref, km_ref, vm_ref):
    order = [(y, xl, c) for y in range(8) for xl in range(2) for c in range(2)]
    for h in range(8):
        for n, (y, xl, c) in enumerate(order):
            km_ref[h, 16 * n : 16 * n + 16, :] = w_ref[c, xl, y, 16 * h : 16 * h + 16, :]
        value = [w_ref[c, xl, y, 128 + 16 * h : 144 + 16 * h, :] for y, xl, c in order]
        vm_ref[h] = jnp.concatenate(value, axis=0).T


def arrange(wide):
    return pl.pallas_call(
        maps_kernel,
        out_shape=(
            jax.ShapeDtypeStruct((8, LAT, 128), BF),
            jax.ShapeDtypeStruct((8, 128, LAT), BF),
        ),
        compiler_params=pltpu.CompilerParams(vmem_limit_bytes=48 * 1024 * 1024),
        name="arrange_maps",
    )(wide)


def project_kernel(x_ref, w_ref, h_ref, d_ref, cos_ref, sin_ref, o_ref):
    tokens = h_ref.shape[0]
    nt = (((1,), (1,)), ((), ()))
    part = lax.dot_general(h_ref[...], d_ref[...], nt, preferred_element_type=F32)
    part = jnp.concatenate([part, jnp.zeros((tokens, ROPE), F32)], axis=1).astype(BF)
    order = [(0, 0), (1, 0), (0, 1), (1, 1)]
    zero = jnp.zeros((32, 128), BF)
    acc = jnp.zeros((tokens, 3 * 128), F32)
    for y in range(8):
        plain = []
        rot_a = []
        rot_b = []
        for c, xl in order:
            plain.append(w_ref[c, xl, y, 0:64, :])
            rot = w_ref[c, xl, y, 64:96, :]
            rot_a += [rot, zero]
            rot_b += [zero, rot]
        weights = jnp.concatenate(
            [
                jnp.concatenate(plain, axis=0),
                jnp.concatenate(rot_a, axis=0),
                jnp.concatenate(rot_b, axis=0),
            ],
            axis=1,
        )
        acc = acc + jnp.dot(x_ref[y, :tokens], weights, preferred_element_type=F32)
    q_plain = acc[:, :128].T
    rot = acc[:, 128:256].T[:ROPE] + acc[:, 256:384].T[ROPE:]
    rot = rot.astype(BF).astype(F32)
    r1 = rot[: ROPE // 2]
    r2 = rot[ROPE // 2 :]
    cosine = cos_ref[...]
    sine = sin_ref[...]
    q_rot = jnp.concatenate([r1 * cosine - r2 * sine, r2 * cosine + r1 * sine], axis=0)
    lane = lax.broadcasted_iota(jnp.int32, (16, tokens), 1) // (tokens // 2)
    row = lax.broadcasted_iota(jnp.int32, (16, tokens), 0)
    which = jnp.where(lane == row, 1.0, 0.0)
    tail = jnp.concatenate([q_plain, q_rot, which], axis=0).astype(BF)
    for i in range(o_ref.shape[0]):
        for k in range(5):
            o_ref[i, 16 * k : 16 * k + 16, :] = part[16 * i : 16 * i + 16, 128 * k : 128 * k + 128]
        o_ref[i, SIDE:, :] = tail


def project(x, wide, own, down, cosine, sine):
    tokens = own.shape[0]
    return pl.pallas_call(
        project_kernel,
        out_shape=jax.ShapeDtypeStruct((8, SIDE + NOPE + ROPE + 16, tokens), BF),
        compiler_params=pltpu.CompilerParams(vmem_limit_bytes=48 * 1024 * 1024),
        name="project_queries",
    )(x, wide, own, down, cosine, sine)


def attn_kernel(q_ref, k_ref, v_ref, km_ref, vm_ref, part_ref, gain_ref, cos_ref, sin_ref, o_ref):
    comp = jnp.zeros((SIDE, 128), F32)
    for i in range(part_ref.shape[0]):
        for j in range(part_ref.shape[1]):
            comp = comp + part_ref[i, j].astype(F32)
    squares = jnp.zeros((16, 128), F32)
    for k in range(4):
        lat = comp[16 * k : 16 * k + 16]
        squares = squares + lat * lat
    scale = lax.rsqrt(jnp.sum(squares, axis=1, keepdims=True) * (1.0 / LAT) + 1e-06)
    fresh = [
        comp[16 * k : 16 * k + 16] * scale * gain_ref[:, 128 * k : 128 * k + 128] for k in range(4)
    ]
    rot = comp[64:80]
    lane = lax.broadcasted_iota(jnp.int32, rot.shape, 1)
    across = jnp.where(lane < 32, pltpu.roll(rot, 96, 1), pltpu.roll(rot, 32, 1))
    fresh.append(rot * cos_ref[...] + across * sin_ref[...])
    fresh = jnp.concatenate(fresh, axis=0).astype(BF)
    q = []
    for h in range(2):
        lat = jnp.dot(
            km_ref[h, 0], q_ref[h, 0, SIDE : SIDE + NOPE, :], preferred_element_type=F32
        ).astype(BF)
        q.append(jnp.concatenate([lat, q_ref[h, 0, SIDE + NOPE :, :]], axis=0))
    q = jnp.concatenate(q, axis=1)
    scores = jnp.dot(k_ref[...], q, preferred_element_type=F32)
    top = jnp.max(scores, axis=0, keepdims=True) * SCALE2
    weights = jnp.exp2(scores * SCALE2 - top)
    total = jnp.sum(weights, axis=0, keepdims=True)
    out = jnp.dot(v_ref[...], weights.astype(BF), preferred_element_type=F32).astype(BF)
    a = jnp.dot(vm_ref[0, 0], out[:, :128], preferred_element_type=F32)
    b = jnp.dot(vm_ref[1, 0], out[:, 128:], preferred_element_type=F32)
    stats = jnp.concatenate(
        split3(top) + split3(total) + [jnp.zeros((10, top.shape[1]), F32)], axis=0
    )
    a = jnp.concatenate([a, stats[:, :128]], axis=0)
    b = jnp.concatenate([b, stats[:, 128:]], axis=0)
    low = lax.broadcasted_iota(jnp.int32, a.shape, 1) < 64
    rows = a.shape[0]
    o_ref[0, 0, :rows, :] = jnp.where(low, a, pltpu.roll(b, 64, 1)).astype(BF)
    o_ref[1, 0, :rows, :] = jnp.where(low, pltpu.roll(a, 64, 1), b).astype(BF)
    o_ref[0, 0, rows:, :] = fresh
    o_ref[1, 0, rows:, :] = fresh


def attend(queries, keys, values_t, key_maps, value_maps, gain, cosine, sine):
    groups, pairs, rows, lanes = queries.shape
    n = keys.shape[0]
    out_rows = 128 + 16 + SIDE
    return pl.pallas_call(
        attn_kernel,
        grid=(pairs,),
        in_specs=[
            pl.BlockSpec((2, 1, rows, lanes), lambda i: (0, i, 0, 0)),
            pl.BlockSpec((n, WIDTH + 16), lambda i: (0, 0)),
            pl.BlockSpec((LAT, n), lambda i: (0, 0)),
            pl.BlockSpec((2, 1, LAT, 128), lambda i: (0, i, 0, 0)),
            pl.BlockSpec((2, 1, 128, LAT), lambda i: (0, i, 0, 0)),
            pl.BlockSpec((groups, pairs, SIDE, lanes), lambda i: (0, 0, 0, 0)),
            pl.BlockSpec((1, LAT), lambda i: (0, 0)),
            pl.BlockSpec((16, 128), lambda i: (0, 0)),
            pl.BlockSpec((16, 128), lambda i: (0, 0)),
        ],
        out_specs=pl.BlockSpec((2, 1, out_rows, lanes), lambda i: (0, i, 0, 0)),
        out_shape=jax.ShapeDtypeStruct((2, pairs, out_rows, lanes), BF),
        compiler_params=pltpu.CompilerParams(vmem_limit_bytes=48 * 1024 * 1024),
        cost_estimate=pl.CostEstimate(
            flops=2 * n * 8 * lanes * (WIDTH + LAT), transcendentals=n * 8 * lanes, bytes_accessed=6 << 20
        ),
        name="cache_attention",
    )(queries, keys, values_t, key_maps, value_maps, queries, gain, cosine, sine)


def merge_kernel(part_ref, q_ref, km_ref, vm_ref, tb_ref, w_ref, o_ref, f_ref):
    parts = part_ref.shape[0]
    base = 128 + 16
    fresh = jnp.concatenate(
        [
            jnp.concatenate(
                [part_ref[i, base + 16 * k : base + 16 * k + 16, :] for k in range(5)], axis=1
            )
            for i in range(parts)
        ],
        axis=0,
    )
    fresh_t = fresh[:, :LAT].astype(F32).T.astype(BF)
    fresh = fresh[:, :WIDTH]
    f_ref[...] = fresh
    low = lax.broadcasted_iota(jnp.int32, (1, q_ref.shape[1]), 1) < 64
    plain = q_ref[:NOPE]
    lat = [jnp.dot(km_ref[h], plain, preferred_element_type=F32) for h in range(2)]
    lat = jnp.where(low, lat[0], lat[1]).astype(BF)
    q = jnp.concatenate([lat, q_ref[NOPE:]], axis=0)
    scores = jnp.dot(fresh, q, preferred_element_type=F32) * SCALE2 + tb_ref[...]
    top = jnp.max(scores, axis=0, keepdims=True)
    tops = []
    sums = []
    for i in range(parts):
        stats = part_ref[i, 128 : 128 + 16, :].astype(F32)
        tops.append(stats[0:1] + stats[1:2] + stats[2:3])
        sums.append(stats[3:4] + stats[4:5] + stats[5:6])
        top = jnp.maximum(top, tops[i])
    weights = jnp.exp2(scores - top)
    total = jnp.sum(weights, axis=0, keepdims=True)
    tree = jnp.dot(fresh_t, weights.astype(BF), preferred_element_type=F32).astype(BF)
    tree = [jnp.dot(vm_ref[h], tree, preferred_element_type=F32) for h in range(2)]
    acc = jnp.where(low, tree[0], tree[1])
    for i in range(parts):
        factor = jnp.exp2(tops[i] - top)
        total = total + sums[i] * factor
        acc = acc + part_ref[i, :128, :].astype(F32) * factor
    head = (acc / total).T.astype(BF)
    n = head.shape[0] // 2
    order = [(y, xl, c) for y in range(8) for xl in range(2) for c in range(2)]
    result = jnp.zeros((n, len(order) * 64), F32)
    for h in range(2):
        project = jnp.concatenate(
            [w_ref[c, xl, y, 64 * h : 64 * (h + 1), :] for y, xl, c in order], axis=0
        )
        result = result + lax.dot_general(
            head[h * n : (h + 1) * n],
            project,
            (((1,), (1,)), ((), ())),
            preferred_element_type=F32,
        )
    o_ref[...] = result.astype(BF)


def merge(parts, q_pair, key_maps, value_maps, tree_bias, late):
    lanes = q_pair.shape[1]
    return pl.pallas_call(
        merge_kernel,
        out_shape=(
            jax.ShapeDtypeStruct((lanes // 2, 2048), BF),
            jax.ShapeDtypeStruct((tree_bias.shape[0], WIDTH), BF),
        ),
        compiler_params=pltpu.CompilerParams(vmem_limit_bytes=48 * 1024 * 1024),
        name="merge_project",
    )(parts, q_pair, key_maps, value_maps, tree_bias, late)


def per_device(
    hidden,
    q_weight,
    dkv_weight,
    latent_gain,
    kvb_weight,
    out_weight,
    cache,
    cache_len,
    draft_count,
    parents,
    accept_node,
    page_table,
):
    reqs, draft = parents.shape
    tokens = reqs * draft
    slots, page_len, width = cache.shape
    mp_rank = lax.axis_index(MP)
    zh = lax.axis_index("zh")
    zl = lax.axis_index("zl")
    cols = dkv_weight.shape[1]
    keys = cache.reshape(slots * page_len, width)
    pair = both(jnp.concatenate([hidden, dkv_weight.T], axis=0), "xh")
    hid = jnp.concatenate([pair[0, :tokens], pair[1, :tokens]], axis=1)
    pack = jnp.concatenate(
        [
            q_weight[:, :NOPE],
            jnp.concatenate([q_weight[:32, NOPE:], q_weight[32:, NOPE:]], axis=1),
            pair[0, tokens:],
            pair[1, tokens:],
            jnp.zeros((12, 128), BF),
        ],
        axis=0,
    )
    wide = lax.all_to_all(jnp.broadcast_to(pack[None], (8,) + pack.shape), "y", 0, 0, tiled=True)
    keys_t, hid = lax.optimization_barrier((keys.T, hid))
    other_t = swap(keys_t, "xh")
    sent = jnp.concatenate([hid, kvb_weight[:, 0, :]], axis=0)
    sent = jnp.broadcast_to(sent[None], (8,) + sent.shape)
    wide, sent = lax.optimization_barrier((wide, sent))
    full_x = lax.all_to_all(sent, Z, 0, 0, tiled=True)
    late, full_x = lax.optimization_barrier((out_weight.T, full_x))
    late = both(late, "zh").reshape(128, 128)
    wide = both(both(wide, "xl"), "c")
    wide, other_t = lax.optimization_barrier((wide, other_t))
    down = wide[..., 96 : 96 + 2 * cols, :].transpose(2, 1, 0, 3, 4).reshape(32, 2, cols, 128)
    down = jnp.concatenate([down[:, 0], down[:, 1]], axis=2).reshape(WIDTH, 256)
    maps = full_x[:, tokens:]
    maps = jnp.concatenate(
        [maps[..., :NOPE].reshape(128, 128), maps[..., NOPE:].reshape(128, 128)], axis=0
    )
    maps = lax.all_to_all(jnp.broadcast_to(maps[None], (8,) + maps.shape), "y", 0, 0, tiled=True)
    linked = jax.vmap(tree_reach)(parents)
    depth = jnp.sum(linked, axis=2) - 1.0
    positions = (cache_len.astype(F32)[:, None] + depth).reshape(1, tokens)
    inverse = 10000.0 ** (-(jnp.arange(ROPE // 2, dtype=F32) * 2.0) / ROPE)
    phase = positions * inverse[:, None]
    cosine = jnp.cos(phase)
    sine = jnp.sin(phase)
    mine = lax.dynamic_slice_in_dim(positions.reshape(tokens), 16 * (zh * 4 + zl), 16)
    mine = mine[:, None] * jnp.concatenate([inverse, inverse])[None, :]
    sign = jnp.where(jnp.arange(ROPE) < ROPE // 2, -1.0, 1.0)[None, :]
    mine_cos = jnp.pad(jnp.cos(mine), ((0, 0), (0, 128 - ROPE)))
    mine_sin = jnp.pad(jnp.sin(mine) * sign, ((0, 0), (0, 128 - ROPE)))
    queries = project(full_x, wide, hid, down, cosine, sine)
    queries, maps, other_t = lax.optimization_barrier((queries, maps, other_t))
    queries = lax.all_to_all(queries, Z, 0, 0, tiled=True)
    late = jnp.broadcast_to(late[None], (8,) + late.shape)
    queries, late = lax.optimization_barrier((queries, late))
    late = lax.all_to_all(late, "y", 0, 0, tiled=True)
    maps = both(both(maps, "xl"), "c")
    slot_base = jnp.stack([mp_rank, mp_rank ^ 1]) * slots
    slot_ids = (slot_base[:, None] + jnp.arange(slots, dtype=jnp.int32)[None, :]).reshape(-1)
    page_ids = jnp.arange(reqs * page_table.shape[1], dtype=jnp.int32)
    place = jnp.sum(
        jnp.where(page_table.reshape(-1)[:, None] == slot_ids[None, :], page_ids[:, None], 0), axis=0
    )
    slot_req = place // page_table.shape[1]
    slot_page = place % page_table.shape[1]
    key_pos = slot_page[:, None] * page_len + jnp.arange(page_len, dtype=jnp.int32)[None, :]
    column = jnp.arange(16, dtype=jnp.int32)
    column_len = jnp.pad(cache_len, (0, 16 - reqs))
    hidden_key = jnp.logical_or(
        slot_req[:, None, None] != column, key_pos[:, :, None] >= column_len
    )
    mask = jnp.where(jnp.logical_and(hidden_key, column < reqs), NEG, 0.0).astype(BF)
    mask = mask.reshape(2 * slots * page_len, 16)
    token_req = jnp.arange(tokens, dtype=jnp.int32) // draft
    accept_hot = (accept_node[:, None] == jnp.arange(draft, dtype=jnp.int32)[None, :]).astype(F32)
    path = jnp.sum(accept_hot[:, :, None] * linked, axis=1)
    write_at = jnp.where(
        path > 0.5, cache_len[:, None] + depth.astype(jnp.int32), -1
    ).reshape(tokens)
    chosen = jnp.logical_and(
        slot_req[:slots, None, None] == token_req, key_pos[:slots, :, None] == write_at
    )
    chosen = chosen.reshape(slots * page_len, tokens).astype(BF)
    all_keys, values_t = prepare(keys, other_t, mask)
    key_maps, value_maps = arrange(maps)
    queries = queries.reshape((2, 4) + queries.shape[1:])
    key_maps = key_maps.reshape((2, 4) + key_maps.shape[1:])
    value_maps = value_maps.reshape((2, 4) + value_maps.shape[1:])
    partial = attend(
        queries, all_keys, values_t, key_maps, value_maps, latent_gain[None, :], mine_cos, mine_sin
    )
    partial, late = lax.optimization_barrier((partial, late))
    late = both(both(late, "xl"), "c")
    partial = lax.all_to_all(
        partial.reshape((8,) + partial.shape[2:]), Z, 0, 0, tiled=True
    )
    q_pair = lax.dynamic_index_in_dim(queries, zl, 1, keepdims=False)
    q_pair = q_pair[:, SIDE : SIDE + NOPE + ROPE]
    q_pair = jnp.where(zh == 0, q_pair[..., :draft], q_pair[..., draft:])
    q_pair = jnp.concatenate([q_pair[0], q_pair[1]], axis=1)
    linked_t = jnp.where(zh == 0, linked[0], linked[1]).T
    blank = jnp.zeros((draft, draft), F32)
    live = jnp.concatenate(
        [jnp.where(zh == 0, linked_t, blank), jnp.where(zh == 0, blank, linked_t)], axis=0
    )
    tree_bias = jnp.where(jnp.concatenate([live, live], axis=1) > 0.5, 0.0, NEG).astype(F32)
    key_pair = lax.dynamic_index_in_dim(key_maps, zl, 1, keepdims=False)
    value_pair = lax.dynamic_index_in_dim(value_maps, zl, 1, keepdims=False)
    projected, fresh = merge(partial, q_pair, key_pair, value_pair, tree_bias, late)
    rows = tokens // 16
    shares = lax.all_to_all(projected.reshape(8, rows, 2048), ("zl", "xh"), 0, 0, tiled=True)
    mine_rows = jnp.sum(shares.astype(F32), axis=0)
    row_index = (mp_rank * rows) % draft + jnp.arange(rows, dtype=jnp.int32)
    row_count = jnp.where(zh == 0, draft_count[0], draft_count[1])
    attended = jnp.where((row_index < row_count)[:, None], mine_rows, 0.0).astype(BF)
    placed = jnp.dot(chosen, fresh, preferred_element_type=F32).astype(BF)
    written = jnp.sum(chosen.astype(F32), axis=1, keepdims=True) > 0.5
    new_cache = jnp.where(written, placed, keys).reshape(cache.shape)
    return (attended, new_cache)


def solution(mesh):
    grid = Mesh(mesh.devices.reshape(8, 2, 2, 2, 4, 2), AXES)
    return jax.shard_map(
        per_device,
        mesh=grid,
        in_specs=(
            P(DP, MP),
            P(DP, MP),
            P(MP, DP),
            P(),
            P(DP, MP, None),
            P(MP, DP),
            P(DP + MP, None, None),
            P(DP),
            P(DP),
            P(DP, None),
            P(DP),
            P(DP, None),
        ),
        out_specs=(P(DP + MP, None), P(DP + MP, None, None)),
        check_vma=False,
    )
```

```python
import jax
import jax.numpy as jnp
from jax import lax
from jax.experimental import pallas as pl
from jax.experimental.pallas import tpu as pltpu
from jax.sharding import Mesh, PartitionSpec as P

NOPE = 128
ROPE = 64
LAT = 512
WIDTH = LAT + ROPE
AXES = ("y", "xl", "c", "zh", "zl", "xh")
DP = ("y", "xl", "c")
MP = ("zh", "zl", "xh")
Z = ("zh", "zl")
SIDE = 80
CHUNKS = 8
SCALE2 = (NOPE + ROPE) ** (-0.5) * 1.4426950408889634
NEG = -1e30
BF = jnp.bfloat16
F32 = jnp.float32


def tree_reach(parent_row):
    count = parent_row.shape[0]
    index = jnp.arange(count, dtype=jnp.int32)
    linked = jnp.logical_or(
        parent_row[:, None] == index[None, :], index[:, None] == index[None, :]
    ).astype(F32)
    for _ in range(max(1, (count - 1).bit_length())):
        linked = jnp.minimum(
            jnp.dot(linked.astype(BF), linked.astype(BF), preferred_element_type=F32), 1.0
        )
    return linked


def swap(x, axis):
    return lax.ppermute(x, axis, [(0, 1), (1, 0)])


def both(x, axis):
    other = swap(x, axis)
    first = lax.axis_index(axis) == 0
    return jnp.stack([jnp.where(first, x, other), jnp.where(first, other, x)])


def split3(v):
    hi = v.astype(BF)
    rest = v - hi.astype(F32)
    mid = rest.astype(BF)
    low = (rest - mid.astype(F32)).astype(BF)
    return [hi.astype(F32), mid.astype(F32), low.astype(F32)]


def prep_kernel(k1_ref, k2t_ref, mask_ref, k_ref, v_ref):
    half = k1_ref.shape[0]
    k_ref[:half, :WIDTH] = k1_ref[...]
    k_ref[half:, :WIDTH] = k2t_ref[...].T
    k_ref[:, WIDTH:] = mask_ref[...]
    v_ref[:, :half] = k1_ref[:, :LAT].T
    v_ref[:, half:] = k2t_ref[:LAT, :]


def prepare(keys, other_t, mask):
    n1 = keys.shape[0]
    return pl.pallas_call(
        prep_kernel,
        out_shape=(
            jax.ShapeDtypeStruct((2 * n1, WIDTH + 16), BF),
            jax.ShapeDtypeStruct((LAT, 2 * n1), BF),
        ),
        compiler_params=pltpu.CompilerParams(vmem_limit_bytes=48 * 1024 * 1024),
        name="prepare_keys",
    )(keys, other_t, mask)


def maps_kernel(w_ref, km_ref, vm_ref):
    order = [(y, xl, c) for y in range(8) for xl in range(2) for c in range(2)]
    for h in range(8):
        for n, (y, xl, c) in enumerate(order):
            km_ref[h, 16 * n : 16 * n + 16, :] = w_ref[c, xl, y, 16 * h : 16 * h + 16, :]
        value = [w_ref[c, xl, y, 128 + 16 * h : 144 + 16 * h, :] for y, xl, c in order]
        vm_ref[h] = jnp.concatenate(value, axis=0).T


def arrange(wide):
    return pl.pallas_call(
        maps_kernel,
        out_shape=(
            jax.ShapeDtypeStruct((8, LAT, 128), BF),
            jax.ShapeDtypeStruct((8, 128, LAT), BF),
        ),
        compiler_params=pltpu.CompilerParams(vmem_limit_bytes=48 * 1024 * 1024),
        name="arrange_maps",
    )(wide)


def project_kernel(x_ref, w_ref, h_ref, d_ref, cos_ref, sin_ref, o_ref):
    tokens = h_ref.shape[0]
    nt = (((1,), (1,)), ((), ()))
    part = lax.dot_general(h_ref[...], d_ref[...], nt, preferred_element_type=F32)
    part = jnp.concatenate([part, jnp.zeros((tokens, ROPE), F32)], axis=1).astype(BF)
    order = [(0, 0), (1, 0), (0, 1), (1, 1)]
    zero = jnp.zeros((32, 128), BF)
    acc = jnp.zeros((tokens, 3 * 128), F32)
    for y in range(8):
        plain = []
        rot_a = []
        rot_b = []
        for c, xl in order:
            plain.append(w_ref[c, xl, y, 0:64, :])
            rot = w_ref[c, xl, y, 64:96, :]
            rot_a += [rot, zero]
            rot_b += [zero, rot]
        weights = jnp.concatenate(
            [
                jnp.concatenate(plain, axis=0),
                jnp.concatenate(rot_a, axis=0),
                jnp.concatenate(rot_b, axis=0),
            ],
            axis=1,
        )
        acc = acc + jnp.dot(x_ref[y, :tokens], weights, preferred_element_type=F32)
    q_plain = acc[:, :128].T
    rot = acc[:, 128:256].T[:ROPE] + acc[:, 256:384].T[ROPE:]
    rot = rot.astype(BF).astype(F32)
    r1 = rot[: ROPE // 2]
    r2 = rot[ROPE // 2 :]
    cosine = cos_ref[...]
    sine = sin_ref[...]
    q_rot = jnp.concatenate([r1 * cosine - r2 * sine, r2 * cosine + r1 * sine], axis=0)
    lane = lax.broadcasted_iota(jnp.int32, (16, tokens), 1) // (tokens // 2)
    row = lax.broadcasted_iota(jnp.int32, (16, tokens), 0)
    which = jnp.where(lane == row, 1.0, 0.0)
    tail = jnp.concatenate([q_plain, q_rot, which], axis=0).astype(BF)
    for i in range(o_ref.shape[0]):
        for k in range(5):
            o_ref[i, 16 * k : 16 * k + 16, :] = part[16 * i : 16 * i + 16, 128 * k : 128 * k + 128]
        o_ref[i, SIDE:, :] = tail


def project(x, wide, own, down, cosine, sine):
    tokens = own.shape[0]
    return pl.pallas_call(
        project_kernel,
        out_shape=jax.ShapeDtypeStruct((8, SIDE + NOPE + ROPE + 16, tokens), BF),
        compiler_params=pltpu.CompilerParams(vmem_limit_bytes=48 * 1024 * 1024),
        name="project_queries",
    )(x, wide, own, down, cosine, sine)


def attn_kernel(q_ref, k_ref, v_ref, km_ref, vm_ref, gain_ref, cos_ref, sin_ref, o_ref, s_ref):
    comp = jnp.zeros((SIDE, 128), F32)
    for i in range(q_ref.shape[0]):
        for j in range(q_ref.shape[1]):
            comp = comp + q_ref[i, j, :SIDE].astype(F32)
    squares = jnp.zeros((16, 128), F32)
    for k in range(4):
        lat = comp[16 * k : 16 * k + 16]
        squares = squares + lat * lat
    scale = lax.rsqrt(jnp.sum(squares, axis=1, keepdims=True) * (1.0 / LAT) + 1e-06)
    fresh = [
        comp[16 * k : 16 * k + 16] * scale * gain_ref[:, 128 * k : 128 * k + 128] for k in range(4)
    ]
    rot = comp[64:80]
    lane = lax.broadcasted_iota(jnp.int32, rot.shape, 1)
    across = jnp.where(lane < 32, pltpu.roll(rot, 96, 1), pltpu.roll(rot, 32, 1))
    fresh.append(rot * cos_ref[...] + across * sin_ref[...])
    fresh = jnp.concatenate(fresh, axis=0).astype(BF)
    step = k_ref.shape[0] // CHUNKS
    pairs = q_ref.shape[1]
    low = lax.broadcasted_iota(jnp.int32, (144, 128), 1) < 64

    def query(i):
        q = []
        for h in range(2):
            lat = jnp.dot(
                km_ref[h, i], q_ref[h, i, SIDE : SIDE + NOPE, :], preferred_element_type=F32
            ).astype(BF)
            q.append(jnp.concatenate([lat, q_ref[h, i, SIDE + NOPE :, :]], axis=0))
        return jnp.concatenate(q, axis=1)

    def score(i, j, q, top):
        part = jnp.dot(k_ref[j * step : (j + 1) * step, :], q, preferred_element_type=F32)
        s_ref[i % 2, j * step : (j + 1) * step, :] = part
        best = jnp.max(part, axis=0, keepdims=True)
        return best if top is None else jnp.maximum(top, best)

    top = None
    q = query(0)
    for j in range(CHUNKS):
        top = score(0, j, q, top)
    for i in range(pairs):
        if i + 1 < pairs:
            q = query(i + 1)
        after = None
        top = top * SCALE2
        total = jnp.zeros((1, 256), F32)
        out = jnp.zeros((LAT, 256), F32)
        for j in range(CHUNKS):
            if i + 1 < pairs:
                after = score(i + 1, j, q, after)
            weights = jnp.exp2(s_ref[i % 2, j * step : (j + 1) * step, :] * SCALE2 - top)
            total = total + jnp.sum(weights, axis=0, keepdims=True)
            out = out + jnp.dot(
                v_ref[:, j * step : (j + 1) * step],
                weights.astype(BF),
                preferred_element_type=F32,
            )
        out = out.astype(BF)
        a = jnp.dot(vm_ref[0, i], out[:, :128], preferred_element_type=F32)
        b = jnp.dot(vm_ref[1, i], out[:, 128:], preferred_element_type=F32)
        stats = jnp.concatenate(
            split3(top) + split3(total) + [jnp.zeros((10, top.shape[1]), F32)], axis=0
        )
        a = jnp.concatenate([a, stats[:, :128]], axis=0)
        b = jnp.concatenate([b, stats[:, 128:]], axis=0)
        o_ref[0, i, :144, :] = jnp.where(low, a, pltpu.roll(b, 64, 1)).astype(BF)
        o_ref[1, i, :144, :] = jnp.where(low, pltpu.roll(a, 64, 1), b).astype(BF)
        o_ref[0, i, 144:, :] = fresh
        o_ref[1, i, 144:, :] = fresh
        top = after


def attend(queries, keys, values_t, key_maps, value_maps, gain, cosine, sine):
    _, pairs, _, lanes = queries.shape
    n = keys.shape[0]
    out_rows = 128 + 16 + SIDE
    return pl.pallas_call(
        attn_kernel,
        out_shape=jax.ShapeDtypeStruct((2, pairs, out_rows, lanes), BF),
        scratch_shapes=[pltpu.VMEM((2, n, 2 * lanes), F32)],
        compiler_params=pltpu.CompilerParams(vmem_limit_bytes=48 * 1024 * 1024),
        cost_estimate=pl.CostEstimate(
            flops=2 * n * 8 * lanes * (WIDTH + LAT), transcendentals=n * 8 * lanes, bytes_accessed=6 << 20
        ),
        name="cache_attention",
    )(queries, keys, values_t, key_maps, value_maps, gain, cosine, sine)


def merge_kernel(part_ref, q_ref, km_ref, vm_ref, tb_ref, w_ref, o_ref, f_ref):
    parts = part_ref.shape[0]
    base = 128 + 16
    fresh = jnp.concatenate(
        [
            jnp.concatenate(
                [part_ref[i, base + 16 * k : base + 16 * k + 16, :] for k in range(5)], axis=1
            )
            for i in range(parts)
        ],
        axis=0,
    )
    fresh_t = fresh[:, :LAT].astype(F32).T.astype(BF)
    fresh = fresh[:, :WIDTH]
    f_ref[...] = fresh
    low = lax.broadcasted_iota(jnp.int32, (1, q_ref.shape[1]), 1) < 64
    plain = q_ref[:NOPE]
    lat = [jnp.dot(km_ref[h], plain, preferred_element_type=F32) for h in range(2)]
    lat = jnp.where(low, lat[0], lat[1]).astype(BF)
    q = jnp.concatenate([lat, q_ref[NOPE:]], axis=0)
    scores = jnp.dot(fresh, q, preferred_element_type=F32) * SCALE2 + tb_ref[...]
    top = jnp.max(scores, axis=0, keepdims=True)
    tops = []
    sums = []
    for i in range(parts):
        stats = part_ref[i, 128 : 128 + 16, :].astype(F32)
        tops.append(stats[0:1] + stats[1:2] + stats[2:3])
        sums.append(stats[3:4] + stats[4:5] + stats[5:6])
        top = jnp.maximum(top, tops[i])
    weights = jnp.exp2(scores - top)
    total = jnp.sum(weights, axis=0, keepdims=True)
    tree = jnp.dot(fresh_t, weights.astype(BF), preferred_element_type=F32).astype(BF)
    tree = [jnp.dot(vm_ref[h], tree, preferred_element_type=F32) for h in range(2)]
    acc = jnp.where(low, tree[0], tree[1])
    for i in range(parts):
        factor = jnp.exp2(tops[i] - top)
        total = total + sums[i] * factor
        acc = acc + part_ref[i, :128, :].astype(F32) * factor
    head = (acc / total).T.astype(BF)
    n = head.shape[0] // 2
    order = [(y, xl, c) for y in range(8) for xl in range(2) for c in range(2)]
    result = jnp.zeros((n, len(order) * 64), F32)
    for h in range(2):
        project = jnp.concatenate(
            [w_ref[c, xl, y, 64 * h : 64 * (h + 1), :] for y, xl, c in order], axis=0
        )
        result = result + lax.dot_general(
            head[h * n : (h + 1) * n],
            project,
            (((1,), (1,)), ((), ())),
            preferred_element_type=F32,
        )
    o_ref[...] = result.astype(BF)


def merge(parts, q_pair, key_maps, value_maps, tree_bias, late):
    lanes = q_pair.shape[1]
    return pl.pallas_call(
        merge_kernel,
        out_shape=(
            jax.ShapeDtypeStruct((lanes // 2, 2048), BF),
            jax.ShapeDtypeStruct((tree_bias.shape[0], WIDTH), BF),
        ),
        compiler_params=pltpu.CompilerParams(vmem_limit_bytes=48 * 1024 * 1024),
        name="merge_project",
    )(parts, q_pair, key_maps, value_maps, tree_bias, late)


def write_kernel(k_ref, c_ref, f_ref, o_ref):
    chosen = c_ref[...]
    placed = jnp.dot(chosen, f_ref[...], preferred_element_type=F32)
    written = jnp.max(chosen.astype(F32), axis=1, keepdims=True) > 0.5
    o_ref[...] = jnp.where(written, placed, k_ref[...].astype(F32)).astype(BF)


def write(keys, chosen, fresh):
    return pl.pallas_call(
        write_kernel,
        out_shape=jax.ShapeDtypeStruct(keys.shape, BF),
        compiler_params=pltpu.CompilerParams(vmem_limit_bytes=48 * 1024 * 1024),
        name="write_entries",
    )(keys, chosen, fresh)


def per_device(
    hidden,
    q_weight,
    dkv_weight,
    latent_gain,
    kvb_weight,
    out_weight,
    cache,
    cache_len,
    draft_count,
    parents,
    accept_node,
    page_table,
):
    reqs, draft = parents.shape
    tokens = reqs * draft
    slots, page_len, width = cache.shape
    mp_rank = lax.axis_index(MP)
    zh = lax.axis_index("zh")
    zl = lax.axis_index("zl")
    cols = dkv_weight.shape[1]
    keys = cache.reshape(slots * page_len, width)
    pair = both(jnp.concatenate([hidden, dkv_weight.T], axis=0), "xh")
    hid = jnp.concatenate([pair[0, :tokens], pair[1, :tokens]], axis=1)
    pack = jnp.concatenate(
        [
            q_weight[:, :NOPE],
            jnp.concatenate([q_weight[:32, NOPE:], q_weight[32:, NOPE:]], axis=1),
            pair[0, tokens:],
            pair[1, tokens:],
            jnp.zeros((12, 128), BF),
        ],
        axis=0,
    )
    pack = jnp.broadcast_to(pack[None], (8,) + pack.shape)
    pack, parents, page_table, cache_t = lax.optimization_barrier((pack, parents, page_table, keys))
    wide = lax.all_to_all(pack, "y", 0, 0, tiled=True)
    other_t = swap(cache_t.T, "xh")
    sent = jnp.concatenate([hid, kvb_weight[:, 0, :]], axis=0)
    sent = jnp.broadcast_to(sent[None], (8,) + sent.shape)
    wide, sent = lax.optimization_barrier((wide, sent))
    full_x = lax.all_to_all(sent, Z, 0, 0, tiled=True)
    late, full_x = lax.optimization_barrier((out_weight.T, full_x))
    late = both(late, "zh").reshape(128, 128)
    wide = both(both(wide, "xl"), "c")
    wide, other_t = lax.optimization_barrier((wide, other_t))
    down = wide[..., 96 : 96 + 2 * cols, :].transpose(2, 1, 0, 3, 4).reshape(32, 2, cols, 128)
    down = jnp.concatenate([down[:, 0], down[:, 1]], axis=2).reshape(WIDTH, 256)
    maps = full_x[:, tokens:]
    maps = jnp.concatenate(
        [maps[..., :NOPE].reshape(128, 128), maps[..., NOPE:].reshape(128, 128)], axis=0
    )
    maps = lax.all_to_all(jnp.broadcast_to(maps[None], (8,) + maps.shape), "y", 0, 0, tiled=True)
    linked = jax.vmap(tree_reach)(parents)
    depth = jnp.sum(linked, axis=2) - 1.0
    positions = (cache_len.astype(F32)[:, None] + depth).reshape(1, tokens)
    inverse = 10000.0 ** (-(jnp.arange(ROPE // 2, dtype=F32) * 2.0) / ROPE)
    phase = positions * inverse[:, None]
    cosine = jnp.cos(phase)
    sine = jnp.sin(phase)
    mine = lax.dynamic_slice_in_dim(positions.reshape(tokens), 16 * (zh * 4 + zl), 16)
    mine = mine[:, None] * jnp.concatenate([inverse, inverse])[None, :]
    sign = jnp.where(jnp.arange(ROPE) < ROPE // 2, -1.0, 1.0)[None, :]
    mine_cos = jnp.pad(jnp.cos(mine), ((0, 0), (0, 128 - ROPE)))
    mine_sin = jnp.pad(jnp.sin(mine) * sign, ((0, 0), (0, 128 - ROPE)))
    slot_base = jnp.stack([mp_rank, mp_rank ^ 1]) * slots
    slot_ids = (slot_base[:, None] + jnp.arange(slots, dtype=jnp.int32)[None, :]).reshape(-1)
    page_ids = jnp.arange(reqs * page_table.shape[1], dtype=jnp.int32)
    place = jnp.sum(
        jnp.where(page_table.reshape(-1)[:, None] == slot_ids[None, :], page_ids[:, None], 0), axis=0
    )
    slot_req = place // page_table.shape[1]
    slot_page = place % page_table.shape[1]
    key_pos = slot_page[:, None] * page_len + jnp.arange(page_len, dtype=jnp.int32)[None, :]
    column = jnp.arange(16, dtype=jnp.int32)
    column_len = jnp.pad(cache_len, (0, 16 - reqs))
    hidden_key = jnp.logical_or(
        slot_req[:, None, None] != column, key_pos[:, :, None] >= column_len
    )
    mask = jnp.where(jnp.logical_and(hidden_key, column < reqs), NEG, 0.0).astype(BF)
    mask = mask.reshape(2 * slots * page_len, 16)
    token_req = jnp.arange(tokens, dtype=jnp.int32) // draft
    accept_hot = (accept_node[:, None] == jnp.arange(draft, dtype=jnp.int32)[None, :]).astype(F32)
    path = jnp.sum(accept_hot[:, :, None] * linked, axis=1)
    write_at = jnp.where(
        path > 0.5, cache_len[:, None] + depth.astype(jnp.int32), -1
    ).reshape(tokens)
    chosen = jnp.logical_and(
        slot_req[:slots, None, None] == token_req, key_pos[:slots, :, None] == write_at
    )
    chosen = chosen.reshape(slots * page_len, tokens).astype(BF)
    all_keys, values_t = prepare(keys, other_t, mask)
    queries = project(full_x, wide, hid, down, cosine, sine)
    late = jnp.broadcast_to(late[None], (8,) + late.shape)
    queries, maps, all_keys, values_t, late = lax.optimization_barrier(
        (queries, maps, all_keys, values_t, late)
    )
    queries = lax.all_to_all(queries, Z, 0, 0, tiled=True)
    queries, late = lax.optimization_barrier((queries, late))
    late = lax.all_to_all(late, "y", 0, 0, tiled=True)
    maps = both(both(maps, "xl"), "c")
    key_maps, value_maps = arrange(maps)
    queries = queries.reshape((2, 4) + queries.shape[1:])
    key_maps = key_maps.reshape((2, 4) + key_maps.shape[1:])
    value_maps = value_maps.reshape((2, 4) + value_maps.shape[1:])
    partial = attend(
        queries, all_keys, values_t, key_maps, value_maps, latent_gain[None, :], mine_cos, mine_sin
    )
    partial, late = lax.optimization_barrier((partial, late))
    late = both(both(late, "xl"), "c")
    partial = lax.all_to_all(
        partial.reshape((8,) + partial.shape[2:]), Z, 0, 0, tiled=True
    )
    q_pair = lax.dynamic_index_in_dim(queries, zl, 1, keepdims=False)
    q_pair = q_pair[:, SIDE : SIDE + NOPE + ROPE]
    q_pair = jnp.where(zh == 0, q_pair[..., :draft], q_pair[..., draft:])
    q_pair = jnp.concatenate([q_pair[0], q_pair[1]], axis=1)
    linked_t = jnp.where(zh == 0, linked[0], linked[1]).T
    blank = jnp.zeros((draft, draft), F32)
    live = jnp.concatenate(
        [jnp.where(zh == 0, linked_t, blank), jnp.where(zh == 0, blank, linked_t)], axis=0
    )
    tree_bias = jnp.where(jnp.concatenate([live, live], axis=1) > 0.5, 0.0, NEG).astype(F32)
    key_pair = lax.dynamic_index_in_dim(key_maps, zl, 1, keepdims=False)
    value_pair = lax.dynamic_index_in_dim(value_maps, zl, 1, keepdims=False)
    projected, fresh = merge(partial, q_pair, key_pair, value_pair, tree_bias, late)
    rows = tokens // 16
    shares = lax.all_to_all(projected.reshape(8, rows, 2048), ("zl", "xh"), 0, 0, tiled=True)
    mine_rows = jnp.sum(shares.astype(F32), axis=0)
    row_index = (mp_rank * rows) % draft + jnp.arange(rows, dtype=jnp.int32)
    row_count = jnp.where(zh == 0, draft_count[0], draft_count[1])
    attended = jnp.where((row_index < row_count)[:, None], mine_rows, 0.0).astype(BF)
    new_cache = write(keys, chosen, fresh).reshape(cache.shape)
    return (attended, new_cache)


def solution(mesh):
    grid = Mesh(mesh.devices.reshape(8, 2, 2, 2, 4, 2), AXES)
    return jax.shard_map(
        per_device,
        mesh=grid,
        in_specs=(
            P(DP, MP),
            P(DP, MP),
            P(MP, DP),
            P(),
            P(DP, MP, None),
            P(MP, DP),
            P(DP + MP, None, None),
            P(DP),
            P(DP),
            P(DP, None),
            P(DP),
            P(DP, None),
        ),
        out_specs=(P(DP + MP, None), P(DP + MP, None, None)),
        check_vma=False,
    )
```

```python
import jax
import jax.numpy as jnp
from jax import lax
from jax.experimental import pallas as pl
from jax.experimental.pallas import tpu as pltpu
from jax.sharding import Mesh, PartitionSpec as P

NOPE = 128
ROPE = 64
LAT = 512
WIDTH = LAT + ROPE
AXES = ("y", "xl", "c", "zh", "zl", "xh")
DP = ("y", "xl", "c")
MP = ("zh", "zl", "xh")
Z = ("zh", "zl")
SIDE = 80
CHUNKS = 8
SCALE2 = (NOPE + ROPE) ** (-0.5) * 1.4426950408889634
NEG = -1e30
BF = jnp.bfloat16
F32 = jnp.float32


def tree_reach(parent_row):
    count = parent_row.shape[0]
    index = jnp.arange(count, dtype=jnp.int32)
    linked = jnp.logical_or(
        parent_row[:, None] == index[None, :], index[:, None] == index[None, :]
    ).astype(F32)
    for _ in range(max(1, (count - 1).bit_length())):
        linked = jnp.minimum(
            jnp.dot(linked.astype(BF), linked.astype(BF), preferred_element_type=F32), 1.0
        )
    return linked


def swap(x, axis):
    return lax.ppermute(x, axis, [(0, 1), (1, 0)])


def both(x, axis):
    other = swap(x, axis)
    first = lax.axis_index(axis) == 0
    return jnp.stack([jnp.where(first, x, other), jnp.where(first, other, x)])


def split3(v):
    hi = v.astype(BF)
    rest = v - hi.astype(F32)
    mid = rest.astype(BF)
    low = (rest - mid.astype(F32)).astype(BF)
    return [hi.astype(F32), mid.astype(F32), low.astype(F32)]


def prep_kernel(k1_ref, k2t_ref, mask_ref, k_ref, v_ref):
    half = k1_ref.shape[0]
    k_ref[:half, :WIDTH] = k1_ref[...]
    k_ref[half:, :WIDTH] = k2t_ref[...].T
    k_ref[:, WIDTH:] = mask_ref[...]
    v_ref[:, :half] = k1_ref[:, :LAT].T
    v_ref[:, half:] = k2t_ref[:LAT, :]


def prepare(keys, other_t, mask):
    n1 = keys.shape[0]
    return pl.pallas_call(
        prep_kernel,
        out_shape=(
            jax.ShapeDtypeStruct((2 * n1, WIDTH + 16), BF),
            jax.ShapeDtypeStruct((LAT, 2 * n1), BF),
        ),
        compiler_params=pltpu.CompilerParams(vmem_limit_bytes=48 * 1024 * 1024),
        name="prepare_keys",
    )(keys, other_t, mask)


def maps_kernel(w_ref, km_ref, vm_ref):
    order = [(y, xl, c) for y in range(8) for xl in range(2) for c in range(2)]
    for h in range(8):
        for n, (y, xl, c) in enumerate(order):
            km_ref[h, 16 * n : 16 * n + 16, :] = w_ref[c, xl, y, 16 * h : 16 * h + 16, :]
        value = [w_ref[c, xl, y, 128 + 16 * h : 144 + 16 * h, :] for y, xl, c in order]
        vm_ref[h] = jnp.concatenate(value, axis=0).T


def arrange(wide):
    return pl.pallas_call(
        maps_kernel,
        out_shape=(
            jax.ShapeDtypeStruct((8, LAT, 128), BF),
            jax.ShapeDtypeStruct((8, 128, LAT), BF),
        ),
        compiler_params=pltpu.CompilerParams(vmem_limit_bytes=48 * 1024 * 1024),
        name="arrange_maps",
    )(wide)


def project_kernel(x_ref, w_ref, h_ref, d_ref, cos_ref, sin_ref, o_ref):
    tokens = h_ref.shape[0]
    nt = (((1,), (1,)), ((), ()))
    part = lax.dot_general(h_ref[...], d_ref[...], nt, preferred_element_type=F32)
    part = jnp.concatenate([part, jnp.zeros((tokens, ROPE), F32)], axis=1).astype(BF)
    order = [(0, 0), (1, 0), (0, 1), (1, 1)]
    zero = jnp.zeros((32, 128), BF)
    acc = jnp.zeros((tokens, 3 * 128), F32)
    for y in range(8):
        plain = []
        rot_a = []
        rot_b = []
        for c, xl in order:
            plain.append(w_ref[c, xl, y, 0:64, :])
            rot = w_ref[c, xl, y, 64:96, :]
            rot_a += [rot, zero]
            rot_b += [zero, rot]
        weights = jnp.concatenate(
            [
                jnp.concatenate(plain, axis=0),
                jnp.concatenate(rot_a, axis=0),
                jnp.concatenate(rot_b, axis=0),
            ],
            axis=1,
        )
        acc = acc + jnp.dot(x_ref[y, :tokens], weights, preferred_element_type=F32)
    q_plain = acc[:, :128].T
    rot = acc[:, 128:256].T[:ROPE] + acc[:, 256:384].T[ROPE:]
    rot = rot.astype(BF).astype(F32)
    r1 = rot[: ROPE // 2]
    r2 = rot[ROPE // 2 :]
    cosine = cos_ref[...]
    sine = sin_ref[...]
    q_rot = jnp.concatenate([r1 * cosine - r2 * sine, r2 * cosine + r1 * sine], axis=0)
    lane = lax.broadcasted_iota(jnp.int32, (16, tokens), 1) // (tokens // 2)
    row = lax.broadcasted_iota(jnp.int32, (16, tokens), 0)
    which = jnp.where(lane == row, 1.0, 0.0)
    tail = jnp.concatenate([q_plain, q_rot, which], axis=0).astype(BF)
    for i in range(o_ref.shape[0]):
        for k in range(5):
            o_ref[i, 16 * k : 16 * k + 16, :] = part[16 * i : 16 * i + 16, 128 * k : 128 * k + 128]
        o_ref[i, SIDE:, :] = tail


def project(x, wide, own, down, cosine, sine):
    tokens = own.shape[0]
    return pl.pallas_call(
        project_kernel,
        out_shape=jax.ShapeDtypeStruct((8, SIDE + NOPE + ROPE + 16, tokens), BF),
        compiler_params=pltpu.CompilerParams(vmem_limit_bytes=48 * 1024 * 1024),
        name="project_queries",
    )(x, wide, own, down, cosine, sine)


def attn_kernel(q_ref, k_ref, v_ref, km_ref, vm_ref, gain_ref, cos_ref, sin_ref, o_ref, s_ref):
    comp = jnp.zeros((SIDE, 128), F32)
    for i in range(q_ref.shape[0]):
        for j in range(q_ref.shape[1]):
            comp = comp + q_ref[i, j, :SIDE].astype(F32)
    squares = jnp.zeros((16, 128), F32)
    for k in range(4):
        lat = comp[16 * k : 16 * k + 16]
        squares = squares + lat * lat
    scale = lax.rsqrt(jnp.sum(squares, axis=1, keepdims=True) * (1.0 / LAT) + 1e-06)
    fresh = [
        comp[16 * k : 16 * k + 16] * scale * gain_ref[:, 128 * k : 128 * k + 128] for k in range(4)
    ]
    rot = comp[64:80]
    lane = lax.broadcasted_iota(jnp.int32, rot.shape, 1)
    across = jnp.where(lane < 32, pltpu.roll(rot, 96, 1), pltpu.roll(rot, 32, 1))
    fresh.append(rot * cos_ref[...] + across * sin_ref[...])
    fresh = jnp.concatenate(fresh, axis=0).astype(BF)
    step = k_ref.shape[0] // CHUNKS
    pairs = q_ref.shape[1]
    low = lax.broadcasted_iota(jnp.int32, (144, 128), 1) < 64

    def query(i):
        q = []
        for h in range(2):
            lat = jnp.dot(
                km_ref[h, i], q_ref[h, i, SIDE : SIDE + NOPE, :], preferred_element_type=F32
            ).astype(BF)
            q.append(jnp.concatenate([lat, q_ref[h, i, SIDE + NOPE :, :]], axis=0))
        return jnp.concatenate(q, axis=1)

    def score(i, j, q, top):
        part = jnp.dot(k_ref[j * step : (j + 1) * step, :], q, preferred_element_type=F32)
        s_ref[i % 2, j * step : (j + 1) * step, :] = part
        best = jnp.max(part, axis=0, keepdims=True)
        return best if top is None else jnp.maximum(top, best)

    top = None
    q = query(0)
    for j in range(CHUNKS):
        top = score(0, j, q, top)
    for i in range(pairs):
        if i + 1 < pairs:
            q = query(i + 1)
        after = None
        top = top * SCALE2
        total = jnp.zeros((1, 256), F32)
        out = jnp.zeros((LAT, 256), F32)
        for j in range(CHUNKS):
            if i + 1 < pairs:
                after = score(i + 1, j, q, after)
            weights = jnp.exp2(s_ref[i % 2, j * step : (j + 1) * step, :] * SCALE2 - top)
            total = total + jnp.sum(weights, axis=0, keepdims=True)
            out = out + jnp.dot(
                v_ref[:, j * step : (j + 1) * step],
                weights.astype(BF),
                preferred_element_type=F32,
            )
        out = out.astype(BF)
        a = jnp.dot(vm_ref[0, i], out[:, :128], preferred_element_type=F32)
        b = jnp.dot(vm_ref[1, i], out[:, 128:], preferred_element_type=F32)
        stats = jnp.concatenate(
            split3(top) + split3(total) + [jnp.zeros((10, top.shape[1]), F32)], axis=0
        )
        a = jnp.concatenate([a, stats[:, :128]], axis=0)
        b = jnp.concatenate([b, stats[:, 128:]], axis=0)
        o_ref[0, i, :144, :] = jnp.where(low, a, pltpu.roll(b, 64, 1)).astype(BF)
        o_ref[1, i, :144, :] = jnp.where(low, pltpu.roll(a, 64, 1), b).astype(BF)
        o_ref[0, i, 144:, :] = fresh
        o_ref[1, i, 144:, :] = fresh
        top = after


def attend(queries, keys, values_t, key_maps, value_maps, gain, cosine, sine):
    _, pairs, _, lanes = queries.shape
    n = keys.shape[0]
    out_rows = 128 + 16 + SIDE
    return pl.pallas_call(
        attn_kernel,
        out_shape=jax.ShapeDtypeStruct((2, pairs, out_rows, lanes), BF),
        scratch_shapes=[pltpu.VMEM((2, n, 2 * lanes), F32)],
        compiler_params=pltpu.CompilerParams(vmem_limit_bytes=48 * 1024 * 1024),
        cost_estimate=pl.CostEstimate(
            flops=2 * n * 8 * lanes * (WIDTH + LAT), transcendentals=n * 8 * lanes, bytes_accessed=6 << 20
        ),
        name="cache_attention",
    )(queries, keys, values_t, key_maps, value_maps, gain, cosine, sine)


def merge_kernel(part_ref, q_ref, km_ref, vm_ref, tb_ref, w_ref, o_ref, f_ref):
    parts = part_ref.shape[0]
    base = 128 + 16
    fresh = jnp.concatenate(
        [
            jnp.concatenate(
                [part_ref[i, base + 16 * k : base + 16 * k + 16, :] for k in range(5)], axis=1
            )
            for i in range(parts)
        ],
        axis=0,
    )
    fresh_t = fresh[:, :LAT].astype(F32).T.astype(BF)
    fresh = fresh[:, :WIDTH]
    f_ref[...] = fresh
    low = lax.broadcasted_iota(jnp.int32, (1, q_ref.shape[1]), 1) < 64
    plain = q_ref[:NOPE]
    lat = [jnp.dot(km_ref[h], plain, preferred_element_type=F32) for h in range(2)]
    lat = jnp.where(low, lat[0], lat[1]).astype(BF)
    q = jnp.concatenate([lat, q_ref[NOPE:]], axis=0)
    scores = jnp.dot(fresh, q, preferred_element_type=F32) * SCALE2 + tb_ref[...]
    top = jnp.max(scores, axis=0, keepdims=True)
    tops = []
    sums = []
    for i in range(parts):
        stats = part_ref[i, 128 : 128 + 16, :].astype(F32)
        tops.append(stats[0:1] + stats[1:2] + stats[2:3])
        sums.append(stats[3:4] + stats[4:5] + stats[5:6])
        top = jnp.maximum(top, tops[i])
    weights = jnp.exp2(scores - top)
    total = jnp.sum(weights, axis=0, keepdims=True)
    tree = jnp.dot(fresh_t, weights.astype(BF), preferred_element_type=F32).astype(BF)
    tree = [jnp.dot(vm_ref[h], tree, preferred_element_type=F32) for h in range(2)]
    acc = jnp.where(low, tree[0], tree[1])
    for i in range(parts):
        factor = jnp.exp2(tops[i] - top)
        total = total + sums[i] * factor
        acc = acc + part_ref[i, :128, :].astype(F32) * factor
    head = (acc / total).T.astype(BF)
    n = head.shape[0] // 2
    order = [(y, xl, c) for y in range(8) for xl in range(2) for c in range(2)]
    result = jnp.zeros((n, len(order) * 64), F32)
    for h in range(2):
        project = jnp.concatenate(
            [w_ref[c, xl, y, 64 * h : 64 * (h + 1), :] for y, xl, c in order], axis=0
        )
        result = result + lax.dot_general(
            head[h * n : (h + 1) * n],
            project,
            (((1,), (1,)), ((), ())),
            preferred_element_type=F32,
        )
    o_ref[...] = result.astype(BF)


def merge(parts, q_pair, key_maps, value_maps, tree_bias, late):
    lanes = q_pair.shape[1]
    return pl.pallas_call(
        merge_kernel,
        out_shape=(
            jax.ShapeDtypeStruct((lanes // 2, 2048), BF),
            jax.ShapeDtypeStruct((tree_bias.shape[0], WIDTH), BF),
        ),
        compiler_params=pltpu.CompilerParams(vmem_limit_bytes=48 * 1024 * 1024),
        name="merge_project",
    )(parts, q_pair, key_maps, value_maps, tree_bias, late)


def write_kernel(k_ref, c_ref, f_ref, o_ref):
    chosen = c_ref[...]
    placed = jnp.dot(chosen, f_ref[...], preferred_element_type=F32)
    written = jnp.max(chosen.astype(F32), axis=1, keepdims=True) > 0.5
    o_ref[...] = jnp.where(written, placed, k_ref[...].astype(F32)).astype(BF)


def write(keys, chosen, fresh):
    return pl.pallas_call(
        write_kernel,
        out_shape=jax.ShapeDtypeStruct(keys.shape, BF),
        compiler_params=pltpu.CompilerParams(vmem_limit_bytes=48 * 1024 * 1024),
        name="write_entries",
    )(keys, chosen, fresh)


def per_device(
    hidden,
    q_weight,
    dkv_weight,
    latent_gain,
    kvb_weight,
    out_weight,
    cache,
    cache_len,
    draft_count,
    parents,
    accept_node,
    page_table,
):
    reqs, draft = parents.shape
    tokens = reqs * draft
    slots, page_len, width = cache.shape
    mp_rank = lax.axis_index(MP)
    zh = lax.axis_index("zh")
    zl = lax.axis_index("zl")
    cols = dkv_weight.shape[1]
    keys = cache.reshape(slots * page_len, width)
    pair = both(jnp.concatenate([hidden, dkv_weight.T], axis=0), "xh")
    hid = jnp.concatenate([pair[0, :tokens], pair[1, :tokens]], axis=1)
    pack = jnp.concatenate(
        [
            q_weight[:, :NOPE],
            jnp.concatenate([q_weight[:32, NOPE:], q_weight[32:, NOPE:]], axis=1),
            pair[0, tokens:],
            pair[1, tokens:],
            jnp.zeros((12, 128), BF),
        ],
        axis=0,
    )
    pack = jnp.broadcast_to(pack[None], (8,) + pack.shape)
    pack, parents, page_table, cache_t = lax.optimization_barrier((pack, parents, page_table, keys))
    wide = lax.all_to_all(pack, "y", 0, 0, tiled=True)
    other_t = swap(cache_t.T, "xh")
    sent = jnp.concatenate([hid, kvb_weight[:, 0, :]], axis=0)
    sent = jnp.broadcast_to(sent[None], (8,) + sent.shape)
    wide, sent = lax.optimization_barrier((wide, sent))
    full_x = lax.all_to_all(sent, Z, 0, 0, tiled=True)
    late, full_x = lax.optimization_barrier((out_weight.T, full_x))
    late = both(late, "zh").reshape(128, 128)
    wide = both(both(wide, "xl"), "c")
    wide, other_t = lax.optimization_barrier((wide, other_t))
    down = wide[..., 96 : 96 + 2 * cols, :].transpose(2, 1, 0, 3, 4).reshape(32, 2, cols, 128)
    down = jnp.concatenate([down[:, 0], down[:, 1]], axis=2).reshape(WIDTH, 256)
    maps = full_x[:, tokens:]
    maps = jnp.concatenate(
        [maps[..., :NOPE].reshape(128, 128), maps[..., NOPE:].reshape(128, 128)], axis=0
    )
    maps = lax.all_to_all(jnp.broadcast_to(maps[None], (8,) + maps.shape), "y", 0, 0, tiled=True)
    linked = jax.vmap(tree_reach)(parents)
    depth = jnp.sum(linked, axis=2) - 1.0
    positions = (cache_len.astype(F32)[:, None] + depth).reshape(1, tokens)
    inverse = 10000.0 ** (-(jnp.arange(ROPE // 2, dtype=F32) * 2.0) / ROPE)
    phase = positions * inverse[:, None]
    cosine = jnp.cos(phase)
    sine = jnp.sin(phase)
    mine = lax.dynamic_slice_in_dim(positions.reshape(tokens), 16 * (zh * 4 + zl), 16)
    mine = mine[:, None] * jnp.concatenate([inverse, inverse])[None, :]
    sign = jnp.where(jnp.arange(ROPE) < ROPE // 2, -1.0, 1.0)[None, :]
    mine_cos = jnp.pad(jnp.cos(mine), ((0, 0), (0, 128 - ROPE)))
    mine_sin = jnp.pad(jnp.sin(mine) * sign, ((0, 0), (0, 128 - ROPE)))
    slot_base = jnp.stack([mp_rank, mp_rank ^ 1]) * slots
    slot_ids = (slot_base[:, None] + jnp.arange(slots, dtype=jnp.int32)[None, :]).reshape(-1)
    page_ids = jnp.arange(reqs * page_table.shape[1], dtype=jnp.int32)
    place = jnp.sum(
        jnp.where(page_table.reshape(-1)[:, None] == slot_ids[None, :], page_ids[:, None], 0), axis=0
    )
    slot_req = place // page_table.shape[1]
    slot_page = place % page_table.shape[1]
    key_pos = slot_page[:, None] * page_len + jnp.arange(page_len, dtype=jnp.int32)[None, :]
    column = jnp.arange(16, dtype=jnp.int32)
    column_len = jnp.pad(cache_len, (0, 16 - reqs))
    hidden_key = jnp.logical_or(
        slot_req[:, None, None] != column, key_pos[:, :, None] >= column_len
    )
    mask = jnp.where(jnp.logical_and(hidden_key, column < reqs), NEG, 0.0).astype(BF)
    mask = mask.reshape(2 * slots * page_len, 16)
    token_req = jnp.arange(tokens, dtype=jnp.int32) // draft
    accept_hot = (accept_node[:, None] == jnp.arange(draft, dtype=jnp.int32)[None, :]).astype(F32)
    path = jnp.sum(accept_hot[:, :, None] * linked, axis=1)
    write_at = jnp.where(
        path > 0.5, cache_len[:, None] + depth.astype(jnp.int32), -1
    ).reshape(tokens)
    chosen = jnp.logical_and(
        slot_req[:slots, None, None] == token_req, key_pos[:slots, :, None] == write_at
    )
    chosen = chosen.reshape(slots * page_len, tokens).astype(BF)
    all_keys, values_t = prepare(keys, other_t, mask)
    queries = project(full_x, wide, hid, down, cosine, sine)
    queries, maps, all_keys, values_t = lax.optimization_barrier(
        (queries, maps, all_keys, values_t)
    )
    queries = lax.all_to_all(queries, Z, 0, 0, tiled=True)
    late = jnp.broadcast_to(late[None], (8,) + late.shape)
    queries, late = lax.optimization_barrier((queries, late))
    late = lax.all_to_all(late, "y", 0, 0, tiled=True)
    maps = both(both(maps, "xl"), "c")
    key_maps, value_maps = arrange(maps)
    queries = queries.reshape((2, 4) + queries.shape[1:])
    key_maps = key_maps.reshape((2, 4) + key_maps.shape[1:])
    value_maps = value_maps.reshape((2, 4) + value_maps.shape[1:])
    partial = attend(
        queries, all_keys, values_t, key_maps, value_maps, latent_gain[None, :], mine_cos, mine_sin
    )
    partial, late = lax.optimization_barrier((partial, late))
    late = both(both(late, "xl"), "c")
    partial = lax.all_to_all(
        partial.reshape((8,) + partial.shape[2:]), Z, 0, 0, tiled=True
    )
    q_pair = lax.dynamic_index_in_dim(queries, zl, 1, keepdims=False)
    q_pair = q_pair[:, SIDE : SIDE + NOPE + ROPE]
    q_pair = jnp.where(zh == 0, q_pair[..., :draft], q_pair[..., draft:])
    q_pair = jnp.concatenate([q_pair[0], q_pair[1]], axis=1)
    linked_t = jnp.where(zh == 0, linked[0], linked[1]).T
    blank = jnp.zeros((draft, draft), F32)
    live = jnp.concatenate(
        [jnp.where(zh == 0, linked_t, blank), jnp.where(zh == 0, blank, linked_t)], axis=0
    )
    tree_bias = jnp.where(jnp.concatenate([live, live], axis=1) > 0.5, 0.0, NEG).astype(F32)
    key_pair = lax.dynamic_index_in_dim(key_maps, zl, 1, keepdims=False)
    value_pair = lax.dynamic_index_in_dim(value_maps, zl, 1, keepdims=False)
    projected, fresh = merge(partial, q_pair, key_pair, value_pair, tree_bias, late)
    rows = tokens // 16
    shares = lax.all_to_all(projected.reshape(8, rows, 2048), ("zl", "xh"), 0, 0, tiled=True)
    mine_rows = jnp.sum(shares.astype(F32), axis=0)
    row_index = (mp_rank * rows) % draft + jnp.arange(rows, dtype=jnp.int32)
    row_count = jnp.where(zh == 0, draft_count[0], draft_count[1])
    attended = jnp.where((row_index < row_count)[:, None], mine_rows, 0.0).astype(BF)
    new_cache = write(keys, chosen, fresh).reshape(cache.shape)
    return (attended, new_cache)


def solution(mesh):
    grid = Mesh(mesh.devices.reshape(8, 2, 2, 2, 4, 2), AXES)
    return jax.shard_map(
        per_device,
        mesh=grid,
        in_specs=(
            P(DP, MP),
            P(DP, MP),
            P(MP, DP),
            P(),
            P(DP, MP, None),
            P(MP, DP),
            P(DP + MP, None, None),
            P(DP),
            P(DP),
            P(DP, None),
            P(DP),
            P(DP, None),
        ),
        out_specs=(P(DP + MP, None), P(DP + MP, None, None)),
        check_vma=False,
    )
```

```python
import jax
import jax.numpy as jnp
from jax import lax
from jax.experimental import pallas as pl
from jax.experimental.pallas import tpu as pltpu
from jax.sharding import Mesh, PartitionSpec as P

NOPE = 128
ROPE = 64
LAT = 512
WIDTH = LAT + ROPE
AXES = ("y", "xl", "c", "zh", "zl", "xh")
DP = ("y", "xl", "c")
MP = ("zh", "zl", "xh")
Z = ("zh", "zl")
SIDE = 80
CHUNKS = 8
SCALE2 = (NOPE + ROPE) ** (-0.5) * 1.4426950408889634
NEG = -1e30
BF = jnp.bfloat16
F32 = jnp.float32


def tree_reach(parent_row):
    count = parent_row.shape[0]
    index = jnp.arange(count, dtype=jnp.int32)
    linked = jnp.logical_or(
        parent_row[:, None] == index[None, :], index[:, None] == index[None, :]
    ).astype(F32)
    for _ in range(max(1, (count - 1).bit_length())):
        linked = jnp.minimum(
            jnp.dot(linked.astype(BF), linked.astype(BF), preferred_element_type=F32), 1.0
        )
    return linked


def swap(x, axis):
    return lax.ppermute(x, axis, [(0, 1), (1, 0)])


def both(x, axis):
    other = swap(x, axis)
    first = lax.axis_index(axis) == 0
    return jnp.stack([jnp.where(first, x, other), jnp.where(first, other, x)])


def split3(v):
    hi = v.astype(BF)
    rest = v - hi.astype(F32)
    mid = rest.astype(BF)
    low = (rest - mid.astype(F32)).astype(BF)
    return [hi.astype(F32), mid.astype(F32), low.astype(F32)]


def prep_kernel(k1_ref, k2t_ref, mask_ref, k_ref, v_ref):
    half = k1_ref.shape[0]
    k_ref[:half, :WIDTH] = k1_ref[...]
    k_ref[half:, :WIDTH] = k2t_ref[...].T
    k_ref[:, WIDTH:] = mask_ref[...]
    v_ref[:, :half] = k1_ref[:, :LAT].T
    v_ref[:, half:] = k2t_ref[:LAT, :]


def prepare(keys, other_t, mask):
    n1 = keys.shape[0]
    return pl.pallas_call(
        prep_kernel,
        out_shape=(
            jax.ShapeDtypeStruct((2 * n1, WIDTH + 16), BF),
            jax.ShapeDtypeStruct((LAT, 2 * n1), BF),
        ),
        compiler_params=pltpu.CompilerParams(vmem_limit_bytes=48 * 1024 * 1024),
        name="prepare_keys",
    )(keys, other_t, mask)


def maps_kernel(w_ref, km_ref, vm_ref):
    order = [(y, xl, c) for y in range(8) for xl in range(2) for c in range(2)]
    for h in range(8):
        for n, (y, xl, c) in enumerate(order):
            km_ref[h, 16 * n : 16 * n + 16, :] = w_ref[c, xl, y, 16 * h : 16 * h + 16, :]
        value = [w_ref[c, xl, y, 128 + 16 * h : 144 + 16 * h, :] for y, xl, c in order]
        vm_ref[h] = jnp.concatenate(value, axis=0).T


def arrange(wide):
    return pl.pallas_call(
        maps_kernel,
        out_shape=(
            jax.ShapeDtypeStruct((8, LAT, 128), BF),
            jax.ShapeDtypeStruct((8, 128, LAT), BF),
        ),
        compiler_params=pltpu.CompilerParams(vmem_limit_bytes=48 * 1024 * 1024),
        name="arrange_maps",
    )(wide)


def project_kernel(x_ref, w_ref, h_ref, d_ref, cos_ref, sin_ref, o_ref):
    tokens = h_ref.shape[0]
    nt = (((1,), (1,)), ((), ()))
    part = lax.dot_general(h_ref[...], d_ref[...], nt, preferred_element_type=F32)
    part = jnp.concatenate([part, jnp.zeros((tokens, ROPE), F32)], axis=1).astype(BF)
    order = [(0, 0), (1, 0), (0, 1), (1, 1)]
    zero = jnp.zeros((32, 128), BF)
    acc = jnp.zeros((tokens, 3 * 128), F32)
    for y in range(8):
        plain = []
        rot_a = []
        rot_b = []
        for c, xl in order:
            plain.append(w_ref[c, xl, y, 0:64, :])
            rot = w_ref[c, xl, y, 64:96, :]
            rot_a += [rot, zero]
            rot_b += [zero, rot]
        weights = jnp.concatenate(
            [
                jnp.concatenate(plain, axis=0),
                jnp.concatenate(rot_a, axis=0),
                jnp.concatenate(rot_b, axis=0),
            ],
            axis=1,
        )
        acc = acc + jnp.dot(x_ref[y, :tokens], weights, preferred_element_type=F32)
    q_plain = acc[:, :128].T
    rot = acc[:, 128:256].T[:ROPE] + acc[:, 256:384].T[ROPE:]
    rot = rot.astype(BF).astype(F32)
    r1 = rot[: ROPE // 2]
    r2 = rot[ROPE // 2 :]
    cosine = cos_ref[...]
    sine = sin_ref[...]
    q_rot = jnp.concatenate([r1 * cosine - r2 * sine, r2 * cosine + r1 * sine], axis=0)
    lane = lax.broadcasted_iota(jnp.int32, (16, tokens), 1) // (tokens // 2)
    row = lax.broadcasted_iota(jnp.int32, (16, tokens), 0)
    which = jnp.where(lane == row, 1.0, 0.0)
    tail = jnp.concatenate([q_plain, q_rot, which], axis=0).astype(BF)
    for i in range(o_ref.shape[0]):
        for k in range(5):
            o_ref[i, 16 * k : 16 * k + 16, :] = part[16 * i : 16 * i + 16, 128 * k : 128 * k + 128]
        o_ref[i, SIDE:, :] = tail


def project(x, wide, own, down, cosine, sine):
    tokens = own.shape[0]
    return pl.pallas_call(
        project_kernel,
        out_shape=jax.ShapeDtypeStruct((8, SIDE + NOPE + ROPE + 16, tokens), BF),
        compiler_params=pltpu.CompilerParams(vmem_limit_bytes=48 * 1024 * 1024),
        name="project_queries",
    )(x, wide, own, down, cosine, sine)


def attn_kernel(q_ref, k_ref, v_ref, km_ref, vm_ref, gain_ref, cos_ref, sin_ref, o_ref, s_ref):
    comp = jnp.zeros((SIDE, 128), F32)
    for i in range(q_ref.shape[0]):
        for j in range(q_ref.shape[1]):
            comp = comp + q_ref[i, j, :SIDE].astype(F32)
    squares = jnp.zeros((16, 128), F32)
    for k in range(4):
        lat = comp[16 * k : 16 * k + 16]
        squares = squares + lat * lat
    scale = lax.rsqrt(jnp.sum(squares, axis=1, keepdims=True) * (1.0 / LAT) + 1e-06)
    fresh = [
        comp[16 * k : 16 * k + 16] * scale * gain_ref[:, 128 * k : 128 * k + 128] for k in range(4)
    ]
    rot = comp[64:80]
    lane = lax.broadcasted_iota(jnp.int32, rot.shape, 1)
    across = jnp.where(lane < 32, pltpu.roll(rot, 96, 1), pltpu.roll(rot, 32, 1))
    fresh.append(rot * cos_ref[...] + across * sin_ref[...])
    fresh = jnp.concatenate(fresh, axis=0).astype(BF)
    step = k_ref.shape[0] // CHUNKS
    pairs = q_ref.shape[1]
    low = lax.broadcasted_iota(jnp.int32, (144, 128), 1) < 64

    def query(i):
        q = []
        for h in range(2):
            lat = jnp.dot(
                km_ref[h, i], q_ref[h, i, SIDE : SIDE + NOPE, :], preferred_element_type=F32
            ).astype(BF)
            q.append(jnp.concatenate([lat, q_ref[h, i, SIDE + NOPE :, :]], axis=0))
        return jnp.concatenate(q, axis=1)

    def score(i, j, q, top):
        part = jnp.dot(k_ref[j * step : (j + 1) * step, :], q, preferred_element_type=F32)
        s_ref[i % 2, j * step : (j + 1) * step, :] = part
        best = jnp.max(part, axis=0, keepdims=True)
        return best if top is None else jnp.maximum(top, best)

    top = None
    q = query(0)
    for j in range(CHUNKS):
        top = score(0, j, q, top)
    for i in range(pairs):
        if i + 1 < pairs:
            q = query(i + 1)
        after = None
        top = top * SCALE2
        total = jnp.zeros((1, 256), F32)
        out = jnp.zeros((LAT, 256), F32)
        for j in range(CHUNKS):
            if i + 1 < pairs:
                after = score(i + 1, j, q, after)
            weights = jnp.exp2(s_ref[i % 2, j * step : (j + 1) * step, :] * SCALE2 - top)
            total = total + jnp.sum(weights, axis=0, keepdims=True)
            out = out + jnp.dot(
                v_ref[:, j * step : (j + 1) * step],
                weights.astype(BF),
                preferred_element_type=F32,
            )
        out = out.astype(BF)
        a = jnp.dot(vm_ref[0, i], out[:, :128], preferred_element_type=F32)
        b = jnp.dot(vm_ref[1, i], out[:, 128:], preferred_element_type=F32)
        stats = jnp.concatenate(
            split3(top) + split3(total) + [jnp.zeros((10, top.shape[1]), F32)], axis=0
        )
        a = jnp.concatenate([a, stats[:, :128]], axis=0)
        b = jnp.concatenate([b, stats[:, 128:]], axis=0)
        o_ref[0, i, :144, :] = jnp.where(low, a, pltpu.roll(b, 64, 1)).astype(BF)
        o_ref[1, i, :144, :] = jnp.where(low, pltpu.roll(a, 64, 1), b).astype(BF)
        o_ref[0, i, 144:, :] = fresh
        o_ref[1, i, 144:, :] = fresh
        top = after


def attend(queries, keys, values_t, key_maps, value_maps, gain, cosine, sine):
    _, pairs, _, lanes = queries.shape
    n = keys.shape[0]
    out_rows = 128 + 16 + SIDE
    return pl.pallas_call(
        attn_kernel,
        out_shape=jax.ShapeDtypeStruct((2, pairs, out_rows, lanes), BF),
        scratch_shapes=[pltpu.VMEM((2, n, 2 * lanes), F32)],
        compiler_params=pltpu.CompilerParams(vmem_limit_bytes=48 * 1024 * 1024),
        cost_estimate=pl.CostEstimate(
            flops=2 * n * 8 * lanes * (WIDTH + LAT), transcendentals=n * 8 * lanes, bytes_accessed=6 << 20
        ),
        name="cache_attention",
    )(queries, keys, values_t, key_maps, value_maps, gain, cosine, sine)


def merge_kernel(part_ref, q_ref, km_ref, vm_ref, tb_ref, w_ref, o_ref, f_ref):
    parts = part_ref.shape[0]
    base = 128 + 16
    fresh = jnp.concatenate(
        [
            jnp.concatenate(
                [part_ref[i, base + 16 * k : base + 16 * k + 16, :] for k in range(5)], axis=1
            )
            for i in range(parts)
        ],
        axis=0,
    )
    fresh_t = fresh[:, :LAT].astype(F32).T.astype(BF)
    fresh = fresh[:, :WIDTH]
    f_ref[...] = fresh
    low = lax.broadcasted_iota(jnp.int32, (1, q_ref.shape[1]), 1) < 64
    plain = q_ref[:NOPE]
    lat = [jnp.dot(km_ref[h], plain, preferred_element_type=F32) for h in range(2)]
    lat = jnp.where(low, lat[0], lat[1]).astype(BF)
    q = jnp.concatenate([lat, q_ref[NOPE:]], axis=0)
    scores = jnp.dot(fresh, q, preferred_element_type=F32) * SCALE2 + tb_ref[...]
    top = jnp.max(scores, axis=0, keepdims=True)
    tops = []
    sums = []
    for i in range(parts):
        stats = part_ref[i, 128 : 128 + 16, :].astype(F32)
        tops.append(stats[0:1] + stats[1:2] + stats[2:3])
        sums.append(stats[3:4] + stats[4:5] + stats[5:6])
        top = jnp.maximum(top, tops[i])
    weights = jnp.exp2(scores - top)
    total = jnp.sum(weights, axis=0, keepdims=True)
    tree = jnp.dot(fresh_t, weights.astype(BF), preferred_element_type=F32).astype(BF)
    tree = [jnp.dot(vm_ref[h], tree, preferred_element_type=F32) for h in range(2)]
    acc = jnp.where(low, tree[0], tree[1])
    for i in range(parts):
        factor = jnp.exp2(tops[i] - top)
        total = total + sums[i] * factor
        acc = acc + part_ref[i, :128, :].astype(F32) * factor
    head = (acc / total).T.astype(BF)
    n = head.shape[0] // 2
    order = [(y, xl, c) for y in range(8) for xl in range(2) for c in range(2)]
    result = jnp.zeros((n, len(order) * 64), F32)
    for h in range(2):
        project = jnp.concatenate(
            [w_ref[c, xl, y, 64 * h : 64 * (h + 1), :] for y, xl, c in order], axis=0
        )
        result = result + lax.dot_general(
            head[h * n : (h + 1) * n],
            project,
            (((1,), (1,)), ((), ())),
            preferred_element_type=F32,
        )
    o_ref[...] = result.astype(BF)


def merge(parts, q_pair, key_maps, value_maps, tree_bias, late):
    lanes = q_pair.shape[1]
    return pl.pallas_call(
        merge_kernel,
        out_shape=(
            jax.ShapeDtypeStruct((lanes // 2, 2048), BF),
            jax.ShapeDtypeStruct((tree_bias.shape[0], WIDTH), BF),
        ),
        compiler_params=pltpu.CompilerParams(vmem_limit_bytes=48 * 1024 * 1024),
        name="merge_project",
    )(parts, q_pair, key_maps, value_maps, tree_bias, late)


def write_kernel(k_ref, c_ref, f_ref, o_ref):
    chosen = c_ref[...]
    placed = jnp.dot(chosen, f_ref[...], preferred_element_type=F32)
    written = jnp.max(chosen.astype(F32), axis=1, keepdims=True) > 0.5
    o_ref[...] = jnp.where(written, placed, k_ref[...].astype(F32)).astype(BF)


def write(keys, chosen, fresh):
    return pl.pallas_call(
        write_kernel,
        out_shape=jax.ShapeDtypeStruct(keys.shape, BF),
        compiler_params=pltpu.CompilerParams(vmem_limit_bytes=48 * 1024 * 1024),
        name="write_entries",
    )(keys, chosen, fresh)


def per_device(
    hidden,
    q_weight,
    dkv_weight,
    latent_gain,
    kvb_weight,
    out_weight,
    cache,
    cache_len,
    draft_count,
    parents,
    accept_node,
    page_table,
):
    reqs, draft = parents.shape
    tokens = reqs * draft
    slots, page_len, width = cache.shape
    mp_rank = lax.axis_index(MP)
    zh = lax.axis_index("zh")
    zl = lax.axis_index("zl")
    cols = dkv_weight.shape[1]
    keys = cache.reshape(slots * page_len, width)
    pair = both(jnp.concatenate([hidden, dkv_weight.T], axis=0), "xh")
    hid = jnp.concatenate([pair[0, :tokens], pair[1, :tokens]], axis=1)
    pack = jnp.concatenate(
        [
            q_weight[:, :NOPE],
            jnp.concatenate([q_weight[:32, NOPE:], q_weight[32:, NOPE:]], axis=1),
            pair[0, tokens:],
            pair[1, tokens:],
            jnp.zeros((12, 128), BF),
        ],
        axis=0,
    )
    pack = jnp.broadcast_to(pack[None], (8,) + pack.shape)
    pack, parents, page_table, cache_t = lax.optimization_barrier((pack, parents, page_table, keys))
    wide = lax.all_to_all(pack, "y", 0, 0, tiled=True)
    other_t = swap(cache_t.T, "xh")
    sent = jnp.concatenate([hid, kvb_weight[:, 0, :]], axis=0)
    sent = jnp.broadcast_to(sent[None], (8,) + sent.shape)
    wide, sent, late = lax.optimization_barrier((wide, sent, out_weight.T))
    full_x = lax.all_to_all(sent, Z, 0, 0, tiled=True)
    late = both(late, "zh").reshape(128, 128)
    late, full_x = lax.optimization_barrier((late, full_x))
    wide = both(both(wide, "xl"), "c")
    wide, other_t = lax.optimization_barrier((wide, other_t))
    down = wide[..., 96 : 96 + 2 * cols, :].transpose(2, 1, 0, 3, 4).reshape(32, 2, cols, 128)
    down = jnp.concatenate([down[:, 0], down[:, 1]], axis=2).reshape(WIDTH, 256)
    maps = full_x[:, tokens:]
    maps = jnp.concatenate(
        [maps[..., :NOPE].reshape(128, 128), maps[..., NOPE:].reshape(128, 128)], axis=0
    )
    maps = lax.all_to_all(jnp.broadcast_to(maps[None], (8,) + maps.shape), "y", 0, 0, tiled=True)
    linked = jax.vmap(tree_reach)(parents)
    depth = jnp.sum(linked, axis=2) - 1.0
    positions = (cache_len.astype(F32)[:, None] + depth).reshape(1, tokens)
    inverse = 10000.0 ** (-(jnp.arange(ROPE // 2, dtype=F32) * 2.0) / ROPE)
    phase = positions * inverse[:, None]
    cosine = jnp.cos(phase)
    sine = jnp.sin(phase)
    mine = lax.dynamic_slice_in_dim(positions.reshape(tokens), 16 * (zh * 4 + zl), 16)
    mine = mine[:, None] * jnp.concatenate([inverse, inverse])[None, :]
    sign = jnp.where(jnp.arange(ROPE) < ROPE // 2, -1.0, 1.0)[None, :]
    mine_cos = jnp.pad(jnp.cos(mine), ((0, 0), (0, 128 - ROPE)))
    mine_sin = jnp.pad(jnp.sin(mine) * sign, ((0, 0), (0, 128 - ROPE)))
    slot_base = jnp.stack([mp_rank, mp_rank ^ 1]) * slots
    slot_ids = (slot_base[:, None] + jnp.arange(slots, dtype=jnp.int32)[None, :]).reshape(-1)
    page_ids = jnp.arange(reqs * page_table.shape[1], dtype=jnp.int32)
    place = jnp.sum(
        jnp.where(page_table.reshape(-1)[:, None] == slot_ids[None, :], page_ids[:, None], 0), axis=0
    )
    slot_req = place // page_table.shape[1]
    slot_page = place % page_table.shape[1]
    key_pos = slot_page[:, None] * page_len + jnp.arange(page_len, dtype=jnp.int32)[None, :]
    column = jnp.arange(16, dtype=jnp.int32)
    column_len = jnp.pad(cache_len, (0, 16 - reqs))
    hidden_key = jnp.logical_or(
        slot_req[:, None, None] != column, key_pos[:, :, None] >= column_len
    )
    mask = jnp.where(jnp.logical_and(hidden_key, column < reqs), NEG, 0.0).astype(BF)
    mask = mask.reshape(2 * slots * page_len, 16)
    token_req = jnp.arange(tokens, dtype=jnp.int32) // draft
    accept_hot = (accept_node[:, None] == jnp.arange(draft, dtype=jnp.int32)[None, :]).astype(F32)
    path = jnp.sum(accept_hot[:, :, None] * linked, axis=1)
    write_at = jnp.where(
        path > 0.5, cache_len[:, None] + depth.astype(jnp.int32), -1
    ).reshape(tokens)
    chosen = jnp.logical_and(
        slot_req[:slots, None, None] == token_req, key_pos[:slots, :, None] == write_at
    )
    chosen = chosen.reshape(slots * page_len, tokens).astype(BF)
    queries = project(full_x, wide, hid, down, cosine, sine)
    queries, maps, other_t = lax.optimization_barrier((queries, maps, other_t))
    queries = lax.all_to_all(queries, Z, 0, 0, tiled=True)
    late = jnp.broadcast_to(late[None], (8,) + late.shape)
    queries, late = lax.optimization_barrier((queries, late))
    late = lax.all_to_all(late, "y", 0, 0, tiled=True)
    maps = both(both(maps, "xl"), "c")
    all_keys, values_t = prepare(keys, other_t, mask)
    key_maps, value_maps = arrange(maps)
    queries = queries.reshape((2, 4) + queries.shape[1:])
    key_maps = key_maps.reshape((2, 4) + key_maps.shape[1:])
    value_maps = value_maps.reshape((2, 4) + value_maps.shape[1:])
    partial = attend(
        queries, all_keys, values_t, key_maps, value_maps, latent_gain[None, :], mine_cos, mine_sin
    )
    partial, late = lax.optimization_barrier((partial, late))
    late = both(both(late, "xl"), "c")
    partial = lax.all_to_all(
        partial.reshape((8,) + partial.shape[2:]), Z, 0, 0, tiled=True
    )
    q_pair = lax.dynamic_index_in_dim(queries, zl, 1, keepdims=False)
    q_pair = q_pair[:, SIDE : SIDE + NOPE + ROPE]
    q_pair = jnp.where(zh == 0, q_pair[..., :draft], q_pair[..., draft:])
    q_pair = jnp.concatenate([q_pair[0], q_pair[1]], axis=1)
    linked_t = jnp.where(zh == 0, linked[0], linked[1]).T
    blank = jnp.zeros((draft, draft), F32)
    live = jnp.concatenate(
        [jnp.where(zh == 0, linked_t, blank), jnp.where(zh == 0, blank, linked_t)], axis=0
    )
    tree_bias = jnp.where(jnp.concatenate([live, live], axis=1) > 0.5, 0.0, NEG).astype(F32)
    key_pair = lax.dynamic_index_in_dim(key_maps, zl, 1, keepdims=False)
    value_pair = lax.dynamic_index_in_dim(value_maps, zl, 1, keepdims=False)
    projected, fresh = merge(partial, q_pair, key_pair, value_pair, tree_bias, late)
    rows = tokens // 16
    shares = lax.all_to_all(projected.reshape(8, rows, 2048), ("zl", "xh"), 0, 0, tiled=True)
    mine_rows = jnp.sum(shares.astype(F32), axis=0)
    row_index = (mp_rank * rows) % draft + jnp.arange(rows, dtype=jnp.int32)
    row_count = jnp.where(zh == 0, draft_count[0], draft_count[1])
    attended = jnp.where((row_index < row_count)[:, None], mine_rows, 0.0).astype(BF)
    new_cache = write(keys, chosen, fresh).reshape(cache.shape)
    return (attended, new_cache)


def solution(mesh):
    grid = Mesh(mesh.devices.reshape(8, 2, 2, 2, 4, 2), AXES)
    return jax.shard_map(
        per_device,
        mesh=grid,
        in_specs=(
            P(DP, MP),
            P(DP, MP),
            P(MP, DP),
            P(),
            P(DP, MP, None),
            P(MP, DP),
            P(DP + MP, None, None),
            P(DP),
            P(DP),
            P(DP, None),
            P(DP),
            P(DP, None),
        ),
        out_specs=(P(DP + MP, None), P(DP + MP, None, None)),
        check_vma=False,
    )
```
